32 devices in a mesh: group: 2 (over y), tm: 4 (over x, core), row: 4 (over z).
Axes of the slice: x: 2, y: 2, z: 4, core: 2. Of those that a mesh axis runs over, the one named last changes fastest.
Arguments:
- traces: bfloat16 [4096, 1024], P('row', ('group', 'tm')), parts along dimension 1, may hold values from -6 to 6
- weights: bfloat16 [4, 4096, 4096], P(None, 'row'), may hold values from -0.09375 to 0.09375
- pattern: int32 [4, 32, 32], replicated, may hold values 0 or 1
- cluster: int32 [4096], replicated, may hold values from 0 to 31
- element_damping_rate: float32 [4096], replicated, may hold values from 0 to 0.034, as said below
- local_step_length: float32 [512], P('tm'), may hold values from 0.4 to 1.9, as said below
- housing_keep_share: float32 [512], P('tm'), may hold values from 0.2 to 1, as said below
- admittance: float32 [4096], replicated, may hold values from 0.5 to 2
Outputs:
- adjoint_state: float32 [4096, 1024], P('row', ('group', 'tm')), parts along dimension 1
- pressure: bfloat16 [4096, 1024], P('row', ('group', 'tm')), parts along dimension 1
The draws below stay inside these ranges and needn't reach their ends.
There are 2 independent parts, one for each index of `group`. The reference program is written for one: setup_inputs(seed, part) draws one part's arguments, and reference() takes and returns one part's arrays. A program takes and returns all parts, laid end to end along the dimension named above; an argument that names none is the same for every part. Nothing has to cross between parts.
Inputs may be any that keep to these rules, and one draw needn't show every extreme that they name: `element_damping_rate`: damping rates, positive. `local_step_length`: positive step lengths. `housing_keep_share`: kept shares, positive.
All inputs are finite; a program needn't handle non-finite values.
Results may differ from the reference program's by a relative error of at most 0.012.
Values may be sent and summed in bfloat16 or wider, within the bound.
No kernel may reach another device: no remote copies, remote signals or barrier semaphores. Data moves between devices by JAX's collectives and lax.ppermute only.
A program may use at most 192 MiB of HBM per device.

```python
import math
import jax
import jax.numpy as jnp
from jax import lax

E = 4096
LAGS = 4
CLUSTERS = 32
TB = 128
STEPS = 512
N_ROW = 4


def draw_element_damping_rate(key, part):
    pick_key, fast_key, slow_key = jax.random.split(key, 3)
    fast_share = 0.5
    chooser = jax.random.uniform(pick_key, (E,), jnp.float32)
    fast_rate = jnp.exp(jax.random.uniform(fast_key, (E,), jnp.float32, math.log(1.0 / 50.0), math.log(1.0 / 30.0)))
    slow_rate = jax.random.uniform(slow_key, (E,), jnp.float32, 0.05, 0.4) / STEPS
    return jnp.where(chooser < fast_share, fast_rate, slow_rate)


def draw_local_step_length(key, part):
    block_key, rough_key = jax.random.split(key, 2)
    level = jnp.exp(jax.random.uniform(block_key, (STEPS // TB,), jnp.float32, math.log(0.6), math.log(1.4)))
    rough = jax.random.uniform(rough_key, (STEPS,), jnp.float32, 0.7, 1.3)
    return jnp.repeat(level, TB, total_repeat_length=STEPS) * rough


def draw_housing_keep_share(key, part):
    place_key, depth_key = jax.random.split(key, 2)
    spots = jax.random.randint(place_key, (3,), 0, STEPS)
    depth = jax.random.uniform(depth_key, (3,), jnp.float32, 0.6, 0.8)
    moment = jnp.arange(STEPS, dtype=jnp.int32)
    struck = moment[:, None] == spots[None, :]
    return jnp.prod(jnp.where(struck, depth[None, :], 1.0), axis=1).astype(jnp.float32)


def place_ends(values, own_key, least, largest):
    index_at = [jax.random.randint(jax.random.fold_in(own_key, axis), (), 0, length) for axis, length in enumerate(values.shape)]
    main_axis = values.shape.index(max(values.shape))
    neighbour = index_at[:main_axis] + [(index_at[main_axis] + 1) % values.shape[main_axis]] + index_at[main_axis + 1:]
    return values.at[tuple(index_at)].set(least).at[tuple(neighbour)].set(largest)


def strengthened(array, own_key, source, target, shards_of, factor):
    owner, partner = [(jnp.arange(array.shape[dim]) // (array.shape[dim] // shards_of)).reshape([-1 if axis == dim else 1 for axis in range(array.ndim)]) for dim in (source, target)]
    chosen = jax.random.permutation(own_key, shards_of)[partner]
    strong = (owner == chosen) | (owner == (partner + shards_of // 2) % shards_of)
    return jnp.where(strong, factor * array, array)


def levels(stream_key, shape, cuts, smallest, top_value):
    gain, own = 1.0, jax.random.fold_in(stream_key, 6)
    for position, blocks in cuts:
        heights = jnp.exp(jax.random.uniform(jax.random.fold_in(own, position), (blocks,), jnp.float32, smallest / len(cuts), top_value / len(cuts)))
        gain = gain * jnp.repeat(heights, shape[position] // blocks).reshape([-1 if axis == position else 1 for axis in range(len(shape))])
    return gain


def normal_values(own_key, shape, scale, bound, shards=(), kind=jnp.bfloat16):
    level = levels(own_key, shape, shards, -0.22, 0.18) if shards else 1.0
    values = jax.random.normal(own_key, shape, jnp.float32) * scale * level
    return jnp.minimum(jnp.maximum(values, -bound), bound).astype(kind)


def bell_draw_with(stream_key, dims, scale, limit, cuts, heavy, held_as=jnp.bfloat16):
    drawn = scale * jax.random.normal(stream_key, dims, jnp.float32)
    if cuts:
        drawn = drawn * levels(stream_key, dims, cuts, -0.22, 0.18)
    return jnp.clip(strengthened(drawn, jax.random.fold_in(stream_key, 3), *heavy), -limit, limit).astype(held_as)


def setup_inputs(seed: int = 0, part: int = 0) -> dict:
    arg_keys = jax.random.split(jax.random.key(seed), 9)
    part_splits = jax.random.split(jax.random.fold_in(arg_keys[8], part), 9)
    return {
        "traces": normal_values(part_splits[0], (E, STEPS), 1.0, 6.0, ((0, 4), (1, 4))),
        "weights": bell_draw_with(arg_keys[1], (LAGS, E, E), (E * LAGS // 2) ** -0.5, 0.09375, ((1, 4),), (1, 2, 4, 2.0)),
        "pattern": place_ends((jax.random.randint(arg_keys[2], (LAGS, CLUSTERS, CLUSTERS), 0, 4) < 3).astype(jnp.int32), jax.random.fold_in(arg_keys[2], 1), 0, 1),
        "cluster": place_ends(jax.random.randint(arg_keys[3], (E,), 0, CLUSTERS), jax.random.fold_in(arg_keys[3], 1), 0, CLUSTERS - 1).astype(jnp.int32),
        "element_damping_rate": draw_element_damping_rate(jax.random.fold_in(arg_keys[8], 71), part),
        "local_step_length": draw_local_step_length(jax.random.fold_in(arg_keys[8], 71), part),
        "housing_keep_share": draw_housing_keep_share(jax.random.fold_in(arg_keys[8], 71), part),
        "admittance": jnp.clip(jnp.exp(jax.random.uniform(arg_keys[7], (E,), jnp.float32, math.log(0.5), math.log(2.0))), 0.5, 2.0),
    }


def lag_kernel(weights, pattern, cluster, lag_index):
    table = pattern[lag_index][cluster[:, None], cluster[None, :]]
    return weights[lag_index] * table.astype(jnp.bfloat16)

def reference(traces, weights, pattern, cluster, element_damping_rate, local_step_length, housing_keep_share, admittance):
    length = traces.shape[1]
    group_rows = E // N_ROW
    kernels = [lag_kernel(weights, pattern, cluster, lag_index) for lag_index in range(LAGS)]
    extended = jnp.concatenate([traces, jnp.zeros((E, LAGS - 1), traces.dtype)], 1)

    def add_group(running, group):
        first_row = (group * group_rows).astype(jnp.int32)
        trace_rows = lax.dynamic_slice_in_dim(extended, first_row, group_rows, 0)
        group_sum = jnp.zeros((E, length), jnp.float32)
        for lag_index in range(LAGS):
            kernel_rows = lax.dynamic_slice_in_dim(kernels[lag_index], first_row, group_rows, 0)
            group_sum = group_sum + jnp.dot(kernel_rows.T, trace_rows[:, lag_index:lag_index + length], preferred_element_type=jnp.float32)
        rounded = lax.optimization_barrier(group_sum.astype(jnp.bfloat16))
        return (running + rounded.astype(jnp.float32), None)
    adjoint_total_sum, _ = lax.scan(add_group, jnp.zeros((E, length), jnp.float32), jnp.arange(N_ROW, dtype=jnp.int32))
    distribute_rows = element_damping_rate[:, None] * local_step_length[None, :]
    keep_fraction = jnp.exp(-distribute_rows) * housing_keep_share[None, :]
    inflow = jnp.sqrt(-jnp.expm1(-2.0 * distribute_rows)) * adjoint_total_sum

    def backward(carried, columns):
        keep_col, inflow_col = columns
        carried = keep_col * carried + inflow_col
        return (carried, carried)
    _, states = lax.scan(backward, jnp.zeros((E,), jnp.float32), (keep_fraction.T, inflow.T), reverse=True)
    adjoint_state = states.T
    driving = (admittance[:, None] * adjoint_state).astype(jnp.bfloat16)
    shifted = jnp.concatenate([jnp.zeros((E, LAGS - 1), jnp.bfloat16), driving], 1)
    pressure = jnp.zeros((E, length), jnp.float32)
    for lag_index in range(LAGS):
        offset = LAGS - 1 - lag_index
        pressure = pressure + jnp.dot(kernels[lag_index], shifted[:, offset:offset + length], preferred_element_type=jnp.float32)
    return (adjoint_state, pressure.astype(jnp.bfloat16))
```

```python
import functools

import jax
import jax.numpy as jnp
from jax import lax
from jax.experimental import pallas as pl
from jax.experimental.pallas import tpu as pltpu
from jax.sharding import PartitionSpec as P

HALO = 16
CHUNKS = 2
VMEM_BYTES = 56 << 20


def carried_in(array, axis, join, neutral):
    count = lax.axis_size(axis)
    place = lax.axis_index(axis)
    ahead = count - 1 - place
    gathered = jax.tree.map(
        lambda a, kind: lax.all_gather(a.astype(kind), axis),
        array,
        jax.tree.map(lambda a: jnp.bfloat16 if a.dtype == jnp.float32 else a.dtype, array),
    )
    state = jax.tree.map(lambda a, e: jnp.zeros_like(a) + jnp.asarray(e, a.dtype), array, neutral)

    def one(hop, state):
        source = count - 1 - hop
        return join(
            state,
            jax.tree.map(
                lambda a, own: lax.dynamic_index_in_dim(a, source, 0, False).astype(own.dtype),
                gathered,
                array,
            ),
        )

    return lax.fori_loop(0, ahead, one, state)


def from_behind(array, axis, by):
    count = lax.axis_size(axis)
    pairs = [(i, i + by) for i in range(count) if 0 <= i + by < count]
    return lax.ppermute(array, axis, pairs)


def lag_kernels(weights, pattern, cluster, first_row):
    local_rows = weights.shape[1]
    own_labels = lax.dynamic_slice_in_dim(cluster, first_row, local_rows, 0)
    labels = jnp.arange(pattern.shape[1], dtype=jnp.int32)
    row_onehot = (own_labels[:, None] == labels[None, :]).astype(jnp.bfloat16)
    column_onehot = (labels[:, None] == cluster[None, :]).astype(jnp.bfloat16)
    kernels = []
    for lag_index in range(weights.shape[0]):
        picked = jnp.dot(
            row_onehot, pattern[lag_index].astype(jnp.bfloat16), preferred_element_type=jnp.float32
        )
        table = jnp.dot(
            picked.astype(jnp.bfloat16), column_onehot, preferred_element_type=jnp.float32
        )
        kernels.append(weights[lag_index] * table.astype(jnp.bfloat16))
    return kernels


def correlate(kernels, extended):
    length = extended.shape[1] - len(kernels) + 1
    running = None
    for lag_index in range(len(kernels)):
        product_term = lax.dot_general(
            kernels[lag_index],
            extended[:, lag_index : lag_index + length],
            (((0,), (0,)), ((), ())),
            preferred_element_type=jnp.float32,
        )
        running = product_term if running is None else running + product_term
    return running


def reconstruct(kernels, extended):
    number_of_lags = len(kernels)
    length = extended.shape[1] - number_of_lags + 1
    running = None
    for lag_index in range(number_of_lags):
        offset = number_of_lags - 1 - lag_index
        product_term = jnp.dot(
            kernels[lag_index],
            extended[:, offset : offset + length],
            preferred_element_type=jnp.float32,
        )
        running = product_term if running is None else running + product_term
    return running


def chain_step(earlier, later):
    return (later[0] * earlier[0], later[1] + later[0] * earlier[1])


def block_recurrence(keep_fraction, inflow):
    def advance(carry, pieces):
        kept_now, state_now = carry
        keep, more = pieces
        state_now = keep * state_now + more
        kept_now = keep * kept_now
        return ((kept_now, state_now), (kept_now, state_now))

    elements = keep_fraction.shape[0]
    start = (jnp.ones((elements,), jnp.float32), jnp.zeros((elements,), jnp.float32))
    _, outputs = lax.scan(advance, start, (keep_fraction.T, inflow.T), reverse=True)
    return (outputs[0].T, outputs[1].T)


def general(
    traces,
    weights,
    pattern,
    cluster,
    element_damping_rate,
    local_step_length,
    housing_keep_share,
    admittance,
):
    local_rows = traces.shape[0]
    length = traces.shape[1]
    number_of_lags = weights.shape[0]
    first_row = lax.axis_index("row") * local_rows
    kernels = lag_kernels(weights, pattern, cluster, first_row)
    trailing = from_behind(traces[:, : number_of_lags - 1], "tm", -1)
    extended = jnp.concatenate([traces, trailing], 1)
    adjoint_sum = lax.psum(correlate(kernels, extended).astype(jnp.bfloat16), "row").astype(
        jnp.float32
    )
    spent = element_damping_rate[:, None] * local_step_length[None, :]
    keep_fraction = jnp.exp(-spent) * housing_keep_share[None, :]
    inflow = jnp.sqrt(-jnp.expm1(-2.0 * spent)) * adjoint_sum
    retained, partial_state = block_recurrence(keep_fraction, inflow)
    neutral = (jnp.ones_like(retained[:, 0]), jnp.zeros_like(partial_state[:, 0]))
    incoming = carried_in((retained[:, 0], partial_state[:, 0]), "tm", chain_step, neutral)
    state = partial_state + retained * incoming[1][:, None]
    driving = (admittance[:, None] * state).astype(jnp.bfloat16)
    leading = from_behind(driving[:, length - number_of_lags + 1 :], "tm", 1)
    pressure = reconstruct(kernels, jnp.concatenate([leading, driving], 1))
    state = lax.dynamic_slice_in_dim(state, first_row, local_rows, 0)
    return (state, pressure.astype(jnp.bfloat16))


def masked(weight, words, bit):
    return jnp.where((words & bit) != 0, weight, jnp.zeros_like(weight))


def correlate_kernel(
    place, traces, partner, ahead, behind, words, bit, weight, o0, o1, o2, o3, steps, lagged, columns
):
    slot = pl.program_id(0)
    lags, rows, _ = weight.shape
    length = traces.shape[1]
    window = lagged.shape[1]
    half = place[1]

    @pl.when(slot == 0)
    def _():
        first = pl.multiple_of(HALO + half * length, HALO)
        second = pl.multiple_of(HALO + (1 - half) * length, HALO)
        steps[0:HALO, :] = ahead[:, 0:rows]
        steps[window : window + HALO, :] = behind[:, 0:rows]
        steps[pl.ds(first, length), :] = traces[...].astype(jnp.float32).T
        steps[pl.ds(second, length), :] = partner[...].astype(jnp.float32).T
        for lag in range(lags):
            lagged[lag] = steps[lag : lag + window, :].astype(jnp.bfloat16)
        columns[...] = words[...].T

    total = None
    for lag in range(lags):
        kernel = masked(weight[lag], columns[:, lag : lag + 1], bit[...])
        term = jnp.dot(lagged[lag], kernel, preferred_element_type=jnp.float32)
        total = term if total is None else total + term
    total = total.astype(jnp.bfloat16)
    for index, out in enumerate((o0, o1, o2, o3)):

        @pl.when(slot == index)
        def _(out=out):
            out[...] = total


def one_less_exp(y):
    series = jnp.ones_like(y)
    for k in range(9, 1, -1):
        series = 1.0 - series * y * (1.0 / k)
    return jnp.where(y < 0.5, y * series, 1.0 - jnp.exp(-y))


def recurrence_kernel(place, own, direct, paired, rate, aux, partial, first):
    window, unit = own.shape
    columns = aux[...].T
    spent = columns[0:window, 0:1] * rate[...]
    total = (
        own[...].astype(jnp.float32)
        + direct[...].astype(jnp.float32)
        + paired[...].astype(jnp.float32)
    )
    kept = jnp.exp(-spent) * columns[0:window, 1:2]
    state = jnp.sqrt(one_less_exp(2.0 * spent)) * total
    index = lax.broadcasted_iota(jnp.int32, (window, unit), 0) & 7
    for shift in (1, 2, 4):
        inside = index < 8 - shift
        later_state = pltpu.roll(state, window - shift, 0)
        later_kept = pltpu.roll(kept, window - shift, 0)
        state = jnp.where(inside, state + kept * later_state, state)
        kept = jnp.where(inside, kept * later_kept, kept)
    carry = jnp.zeros((1, unit), jnp.float32)
    for group in range(window // 8 - 1, -1, -1):
        rows = slice(group * 8, group * 8 + 8)
        block = state[rows] + kept[rows] * carry
        partial[rows, :] = block
        carry = block[0:1]
        if group * 8 == HALO:
            first[...] = jnp.broadcast_to(carry, first.shape)


def finish_kernel(place, partial, incoming, rate, admittance, aux, drive, mine, theirs, states):
    window, unit = partial.shape
    length = mine.shape[1]
    half = place[1]
    columns = aux[...].T
    reach = jnp.exp(-(columns[0:window, 2:3] * rate[...])) * columns[0:window, 3:4]
    state = partial[...] + reach * incoming[0:1, :]
    drive[...] = (admittance[...] * state).astype(jnp.bfloat16)
    states[...] = state
    first = pl.multiple_of(HALO + half * length, HALO)
    second = pl.multiple_of(HALO + (1 - half) * length, HALO)
    mine[...] = states[pl.ds(first, length), :].T
    theirs[...] = states[pl.ds(second, length), :].T


def reconstruct_kernel(last, place, d0, d1, d2, d3, words, bit, weight, *refs):
    if last:
        before, keep, send, total, steps, lagged, columns = refs
    else:
        keep, steps, lagged, columns = refs
        before, total = None, keep
    slot = pl.program_id(0)
    lags, rows, unit = weight.shape
    width = total.shape[1]
    window = d0.shape[0]

    @pl.when(slot == 0)
    def _():
        columns[...] = words[...].T
        total[...] = jnp.zeros_like(total) if before is None else before[...]

    for index, drive in enumerate((d0, d1, d2, d3)):

        @pl.when(slot == index)
        def _(drive=drive):
            steps[...] = drive[...].astype(jnp.float32)

    for lag in range(lags):
        lagged[lag] = steps[HALO - lag : HALO - lag + width, :].astype(jnp.bfloat16)
    added = None
    for lag in range(lags):
        kernel = masked(weight[lag], columns[:, lag : lag + 1], bit[...])
        term = lax.dot_general(
            kernel, lagged[lag], (((1,), (1,)), ((), ())), preferred_element_type=jnp.float32
        )
        added = term if added is None else added + term
    total[...] += added
    if last:
        length = width // 2

        @pl.when(slot == 3)
        def _():
            first = pl.multiple_of(place[1] * length, length)
            second = pl.multiple_of((1 - place[1]) * length, length)
            keep[...] = total[:, pl.ds(first, length)]
            send[...] = total[:, pl.ds(second, length)].astype(send.dtype)


def whole(shape):
    return pl.BlockSpec(shape, lambda slot, place: (0,) * len(shape))


def call(kernel, name, grid, in_specs, out_specs, out_shape, scratch, flops, moved):
    return pl.pallas_call(
        kernel,
        out_shape=out_shape,
        grid_spec=pltpu.PrefetchScalarGridSpec(
            num_scalar_prefetch=1,
            grid=(grid,),
            in_specs=in_specs,
            out_specs=out_specs,
            scratch_shapes=scratch,
        ),
        cost_estimate=pl.CostEstimate(flops=flops, bytes_accessed=moved, transcendentals=0),
        compiler_params=pltpu.CompilerParams(vmem_limit_bytes=VMEM_BYTES),
        name=name,
    )


def paired(
    traces,
    weights,
    pattern,
    cluster,
    element_damping_rate,
    local_step_length,
    housing_keep_share,
    admittance,
):
    rows, length = traces.shape
    lags, _, elements = weights.shape
    window = HALO + 2 * length
    unit = rows // (2 * CHUNKS)
    row = lax.axis_index("row")
    slab = lax.axis_index("tm")
    half = slab % 2
    place = jnp.stack([row, half]).astype(jnp.int32)
    f32, bf16 = jnp.float32, jnp.bfloat16
    tm_count = lax.axis_size("tm")
    swap = [(i, i ^ 1) for i in range(tm_count)]
    near = [(i, i + 1 if i % 2 else i - 1) for i in range(tm_count)]
    near = [(i, j) for i, j in near if 0 <= j < tm_count]
    far = [(i, i + 2 if i % 2 else i - 2) for i in range(tm_count)]
    far = [(i, j) for i, j in far if 0 <= j < tm_count]

    partner = lax.ppermute(traces, "tm", swap)
    clocks = jnp.stack([local_step_length, housing_keep_share])
    partner_clocks = lax.ppermute(clocks, "tm", swap)
    odd = half == 1
    edge = jnp.where(odd, traces[:, length - HALO :], traces[:, :HALO]).astype(f32).T
    edge_clocks = jnp.where(odd, clocks[:, length - HALO :], clocks[:, :HALO]).T
    edge = jnp.concatenate([edge, edge_clocks, jnp.zeros((HALO, 126), f32)], 1)
    got_near = lax.ppermute(edge, "tm", near)
    got_far = lax.ppermute(edge, "tm", far)
    ahead = jnp.where(odd, got_far, got_near)
    behind = jnp.where(odd, got_near, got_far)

    words_by_row = (pattern << jnp.arange(pattern.shape[2], dtype=jnp.int32)).sum(2)
    own_labels = lax.dynamic_slice_in_dim(cluster, row * rows, rows, 0)
    hit = own_labels[None, :] == jnp.arange(pattern.shape[1], dtype=jnp.int32)[:, None]
    words = jnp.where(hit[None], words_by_row[:, :, None], 0).sum(1)
    words = jnp.concatenate([words, jnp.zeros((8 - lags, rows), jnp.int32)], 0)
    bit = (jnp.int32(1) << cluster)[None, :]
    rate = element_damping_rate[None, :]
    gain = admittance[None, :]

    first_clocks = jnp.where(odd, partner_clocks, clocks)
    second_clocks = jnp.where(odd, clocks, partner_clocks)
    clock = jnp.concatenate([ahead[:, rows : rows + 2].T, first_clocks, second_clocks], 1)
    at = jnp.arange(window, dtype=jnp.int32)
    from_here = at[:, None] <= at[None, :]
    spans = jnp.where(from_here, clock[0][None, :], 0.0).sum(1)
    shares = jnp.where(from_here, clock[1][None, :], 1.0).prod(1)
    aux = jnp.concatenate([clock, spans[None], shares[None], jnp.zeros((4, window), f32)], 0)
    aux = jnp.concatenate([aux, jnp.zeros((8, -window % 128), f32)], 1)

    def slot_block(chunk):
        return lambda slot, place: (
            (jnp.bitwise_xor(place[0], slot) * 2 + place[1]) * CHUNKS + chunk
        )

    def weight_spec(chunk):
        block = slot_block(chunk)
        return pl.BlockSpec((lags, rows, unit), lambda slot, place: (0, 0, block(slot, place)))

    def row_spec(chunk, own=False):
        block = slot_block(chunk)
        return pl.BlockSpec(
            (1, unit), lambda slot, place: (0, block(0 if own else slot, place))
        )

    strip = jax.ShapeDtypeStruct((window, unit), bf16)
    share_bytes = 4 * lags * rows * unit * 2
    share_flops = 2 * 4 * lags * rows * unit * window

    def correlated(chunk):
        return call(
            correlate_kernel,
            "correlate",
            4,
            [
                whole((rows, length)),
                whole((rows, length)),
                whole((HALO, rows + 128)),
                whole((HALO, rows + 128)),
                whole((8, rows)),
                row_spec(chunk),
                weight_spec(chunk),
            ],
            [whole((window, unit))] * 4,
            [strip] * 4,
            [
                pltpu.VMEM((window + HALO, rows), f32),
                pltpu.VMEM((lags, window, rows), bf16),
                pltpu.VMEM((rows, 8), jnp.int32),
            ],
            share_flops,
            share_bytes,
        )(place, traces, partner, ahead, behind, words, bit, weights)

    def over_row(array, by):
        return lax.ppermute(array, "row", [(i, i ^ by) for i in range(4)])

    def summed(parts):
        o0, o1, o2, o3 = parts
        s3 = over_row(o3, 1)
        s1 = over_row(o1, 1)
        pair = (o2.astype(f32) + s3.astype(f32)).astype(bf16)
        return o0, s1, over_row(pair, 2)

    def recurrence(chunk, terms):
        return call(
            recurrence_kernel,
            "recurrence",
            1,
            [whole((window, unit))] * 3 + [row_spec(chunk, True), whole(aux.shape)],
            [whole((window, unit)), whole((8, unit))],
            [jax.ShapeDtypeStruct((window, unit), f32), jax.ShapeDtypeStruct((8, unit), f32)],
            [],
            window * unit * 40,
            window * unit * 10,
        )(place, *terms, rate, aux)

    def finished(chunk, partial, incoming):
        piece = jax.ShapeDtypeStruct((unit, length), f32)
        return call(
            finish_kernel,
            "finish",
            1,
            [whole((window, unit)), whole((8, unit))]
            + [row_spec(chunk, True)] * 2
            + [whole(aux.shape)],
            [whole((window, unit)), whole((unit, length)), whole((unit, length))],
            [strip, piece, piece],
            [pltpu.VMEM((window, unit), f32)],
            window * unit * 20,
            window * unit * 12,
        )(place, partial, incoming, rate, gain, aux)

    def reconstructed(chunk, drives, before):
        last = before is not None
        wide = whole((rows, 2 * length))
        scratch = [
            pltpu.VMEM((window, unit), f32),
            pltpu.VMEM((lags, 2 * length, unit), bf16),
            pltpu.VMEM((rows, 8), jnp.int32),
        ]
        if last:
            out_specs = [whole((rows, length))] * 2
            out_shape = [jax.ShapeDtypeStruct((rows, length), f32)] * 2
            out_shape[1] = jax.ShapeDtypeStruct((rows, length), bf16)
            scratch = [pltpu.VMEM((rows, 2 * length), f32)] + scratch
        else:
            out_specs = wide
            out_shape = jax.ShapeDtypeStruct((rows, 2 * length), f32)
        return call(
            functools.partial(reconstruct_kernel, last),
            "reconstruct",
            4,
            [whole((window, unit))] * 4
            + [whole((8, rows)), row_spec(chunk), weight_spec(chunk)]
            + ([wide] if last else []),
            out_specs,
            out_shape,
            scratch,
            share_flops,
            share_bytes,
        )(place, *drives, words, bit, weights, *([before] if last else []))

    parts = [correlated(chunk) for chunk in range(CHUNKS)]
    states, drives = [], []
    for chunk in range(CHUNKS):
        partial, first = recurrence(chunk, summed(parts[chunk]))
        incoming = lax.ppermute(first, "tm", [(i, i - 2) for i in range(2, tm_count)])
        drive, mine, theirs = finished(chunk, partial, incoming)
        d1 = over_row(drive, 1)
        d2 = over_row(drive, 2)
        d3 = over_row(d2, 1)
        drives.append((drive, d1, d2, d3))
        states.append((mine, lax.ppermute(theirs, "tm", swap)))
    held = None
    for chunk in range(CHUNKS):
        held = reconstructed(chunk, drives[chunk], held)
    keep, send = held
    pressure = keep + lax.ppermute(send, "tm", swap).astype(f32)
    mine = jnp.concatenate([s[0] for s in states], 0)
    other = jnp.concatenate([s[1] for s in states], 0)
    state = jnp.where(
        odd, jnp.concatenate([other, mine], 0), jnp.concatenate([mine, other], 0)
    )
    return (state, pressure.astype(bf16))


def local(traces, weights, pattern, *rest):
    rows, length = traces.shape
    fits = (
        lax.axis_size("row") == 4
        and lax.axis_size("tm") == 4
        and length == 128
        and rows % (256 * CHUNKS) == 0
        and weights.shape[0] <= 8
        and pattern.shape[1] <= 32
    )
    return (paired if fits else general)(traces, weights, pattern, *rest)


def solution(mesh):
    placed = (P("row", ("group", "tm")), P(None, "row", None), P(), P(), P(), P("tm"), P("tm"), P())
    return jax.shard_map(
        local,
        mesh=mesh,
        in_specs=placed,
        out_specs=(P("row", ("group", "tm")), P("row", ("group", "tm"))),
        check_vma=False,
    )
```

```python
import functools

import jax
import jax.numpy as jnp
from jax import lax
from jax.experimental import pallas as pl
from jax.experimental.pallas import tpu as pltpu
from jax.sharding import PartitionSpec as P

HALO = 16
CHUNKS = 2
VMEM_BYTES = 20 << 20


def carried_in(array, axis, join, neutral):
    count = lax.axis_size(axis)
    place = lax.axis_index(axis)
    ahead = count - 1 - place
    gathered = jax.tree.map(
        lambda a, kind: lax.all_gather(a.astype(kind), axis),
        array,
        jax.tree.map(lambda a: jnp.bfloat16 if a.dtype == jnp.float32 else a.dtype, array),
    )
    state = jax.tree.map(lambda a, e: jnp.zeros_like(a) + jnp.asarray(e, a.dtype), array, neutral)

    def one(hop, state):
        source = count - 1 - hop
        return join(
            state,
            jax.tree.map(
                lambda a, own: lax.dynamic_index_in_dim(a, source, 0, False).astype(own.dtype),
                gathered,
                array,
            ),
        )

    return lax.fori_loop(0, ahead, one, state)


def from_behind(array, axis, by):
    count = lax.axis_size(axis)
    pairs = [(i, i + by) for i in range(count) if 0 <= i + by < count]
    return lax.ppermute(array, axis, pairs)


def lag_kernels(weights, pattern, cluster, first_row):
    local_rows = weights.shape[1]
    own_labels = lax.dynamic_slice_in_dim(cluster, first_row, local_rows, 0)
    labels = jnp.arange(pattern.shape[1], dtype=jnp.int32)
    row_onehot = (own_labels[:, None] == labels[None, :]).astype(jnp.bfloat16)
    column_onehot = (labels[:, None] == cluster[None, :]).astype(jnp.bfloat16)
    kernels = []
    for lag_index in range(weights.shape[0]):
        picked = jnp.dot(
            row_onehot, pattern[lag_index].astype(jnp.bfloat16), preferred_element_type=jnp.float32
        )
        table = jnp.dot(
            picked.astype(jnp.bfloat16), column_onehot, preferred_element_type=jnp.float32
        )
        kernels.append(weights[lag_index] * table.astype(jnp.bfloat16))
    return kernels


def correlate(kernels, extended):
    length = extended.shape[1] - len(kernels) + 1
    running = None
    for lag_index in range(len(kernels)):
        product_term = lax.dot_general(
            kernels[lag_index],
            extended[:, lag_index : lag_index + length],
            (((0,), (0,)), ((), ())),
            preferred_element_type=jnp.float32,
        )
        running = product_term if running is None else running + product_term
    return running


def reconstruct(kernels, extended):
    number_of_lags = len(kernels)
    length = extended.shape[1] - number_of_lags + 1
    running = None
    for lag_index in range(number_of_lags):
        offset = number_of_lags - 1 - lag_index
        product_term = jnp.dot(
            kernels[lag_index],
            extended[:, offset : offset + length],
            preferred_element_type=jnp.float32,
        )
        running = product_term if running is None else running + product_term
    return running


def chain_step(earlier, later):
    return (later[0] * earlier[0], later[1] + later[0] * earlier[1])


def block_recurrence(keep_fraction, inflow):
    def advance(carry, pieces):
        kept_now, state_now = carry
        keep, more = pieces
        state_now = keep * state_now + more
        kept_now = keep * kept_now
        return ((kept_now, state_now), (kept_now, state_now))

    elements = keep_fraction.shape[0]
    start = (jnp.ones((elements,), jnp.float32), jnp.zeros((elements,), jnp.float32))
    _, outputs = lax.scan(advance, start, (keep_fraction.T, inflow.T), reverse=True)
    return (outputs[0].T, outputs[1].T)


def general(
    traces,
    weights,
    pattern,
    cluster,
    element_damping_rate,
    local_step_length,
    housing_keep_share,
    admittance,
):
    local_rows = traces.shape[0]
    length = traces.shape[1]
    number_of_lags = weights.shape[0]
    first_row = lax.axis_index("row") * local_rows
    kernels = lag_kernels(weights, pattern, cluster, first_row)
    trailing = from_behind(traces[:, : number_of_lags - 1], "tm", -1)
    extended = jnp.concatenate([traces, trailing], 1)
    adjoint_sum = lax.psum(correlate(kernels, extended).astype(jnp.bfloat16), "row").astype(
        jnp.float32
    )
    spent = element_damping_rate[:, None] * local_step_length[None, :]
    keep_fraction = jnp.exp(-spent) * housing_keep_share[None, :]
    inflow = jnp.sqrt(-jnp.expm1(-2.0 * spent)) * adjoint_sum
    retained, partial_state = block_recurrence(keep_fraction, inflow)
    neutral = (jnp.ones_like(retained[:, 0]), jnp.zeros_like(partial_state[:, 0]))
    incoming = carried_in((retained[:, 0], partial_state[:, 0]), "tm", chain_step, neutral)
    state = partial_state + retained * incoming[1][:, None]
    driving = (admittance[:, None] * state).astype(jnp.bfloat16)
    leading = from_behind(driving[:, length - number_of_lags + 1 :], "tm", 1)
    pressure = reconstruct(kernels, jnp.concatenate([leading, driving], 1))
    state = lax.dynamic_slice_in_dim(state, first_row, local_rows, 0)
    return (state, pressure.astype(jnp.bfloat16))


def setup_kernel(
    traces_in,
    length_in,
    share_in,
    pattern_in,
    cluster_in,
    edge,
    clocks,
    columns,
    bits,
    traces,
    turned,
    pattern,
    cluster,
    ready,
):
    rows, length = traces.shape
    lags, kinds, _ = pattern.shape
    row, odd = lax.axis_index("row"), lax.axis_index("tm") % 2
    moves = (
        (traces_in, traces),
        (length_in, clocks.at[0:1, :]),
        (share_in, clocks.at[1:2, :]),
        (pattern_in, pattern),
        (cluster_in, cluster),
    )
    clocks[...] = jnp.zeros_like(clocks)
    copies = [
        pltpu.make_async_copy(source, target, ready.at[index])
        for index, (source, target) in enumerate(moves)
    ]
    for copy in copies:
        copy.start()
    for copy in copies:
        copy.wait()
    turned[:, 0:rows] = traces[...].astype(jnp.float32).T
    turned[:, rows:] = jnp.zeros((length, 128), jnp.float32)
    turned[:, rows : rows + 8] = clocks[...].T
    edge[...] = turned[pl.ds(pl.multiple_of(odd * (length - HALO), HALO), HALO), :]

    bits[...] = jnp.int32(1) << cluster[...]
    labels = cluster[:, pl.ds(pl.multiple_of(row * rows, rows), rows)]
    hit = lax.broadcasted_iota(jnp.int32, (kinds, rows), 0) == labels
    places = lax.broadcasted_iota(jnp.int32, (kinds, pattern.shape[2]), 1)
    found = []
    for lag in range(lags):
        word = (pattern[lag] << places).sum(1, keepdims=True)
        found.append(jnp.where(hit, word, 0).sum(0, keepdims=True))
    found = jnp.concatenate(found + [jnp.zeros((8 - lags, rows), jnp.int32)], 0)
    columns[...] = found.T


def mask_kernel(chunk, columns, bits, weights, kernels, spread, arrived):
    lags, rows, _ = weights.shape
    unit = kernels.shape[1] // 4
    row, half = lax.axis_index("row"), lax.axis_index("tm") % 2

    def start_of(slot):
        owner = jnp.bitwise_xor(row, slot)
        return pl.multiple_of(((owner * 2 + half) * CHUNKS + chunk) * unit, unit)

    def fetch(lag, slot):
        return pltpu.make_async_copy(
            weights.at[lag, :, pl.ds(start_of(slot), unit)],
            kernels.at[pl.ds(lag * rows, rows), pl.ds(slot * unit, unit)],
            arrived.at[slot, lag],
        )

    blocks = [(lag, slot) for lag in range(lags) for slot in range(4)]
    for block in blocks:
        fetch(*block).start()
    picked = [bits[:, pl.ds(start_of(slot), unit)] for slot in range(4)]
    for lag, slot in blocks:
        if slot == 0:
            spread[...] = jnp.broadcast_to(columns[:, lag : lag + 1], (rows, 128))
        fetch(lag, slot).wait()
        for at in range(0, unit, 128):
            place = slice(lag * rows, lag * rows + rows)
            part = slice(slot * unit + at, slot * unit + at + 128)
            weight = kernels[place, part]
            keep = (spread[...] & picked[slot][:, at : at + 128]) != 0
            kernels[place, part] = jnp.where(keep, weight, jnp.zeros_like(weight))


def correlate_kernel(own, partner_in, near, far, kernels, *refs):
    *outs, lagged, steps, traces, partner, ready = refs
    rows, length = traces.shape
    window = lagged.shape[0]
    lags = lagged.shape[1] // rows
    unit = outs[0].shape[1]
    half = lax.axis_index("tm") % 2
    copies = [
        pltpu.make_async_copy(own, traces, ready.at[0]),
        pltpu.make_async_copy(partner_in, partner, ready.at[1]),
    ]
    for copy in copies:
        copy.start()
    odd = half == 1
    first = pl.multiple_of(HALO + half * length, HALO)
    second = pl.multiple_of(HALO + (1 - half) * length, HALO)
    steps[0:HALO, :] = jnp.where(odd, far[:, 0:rows], near[:, 0:rows])
    steps[window : window + HALO, :] = jnp.where(odd, near[:, 0:rows], far[:, 0:rows])
    copies[0].wait()
    steps[pl.ds(first, length), :] = traces[...].astype(jnp.float32).T
    copies[1].wait()
    steps[pl.ds(second, length), :] = partner[...].astype(jnp.float32).T
    for lag in range(lags):
        part = slice(lag * rows, lag * rows + rows)
        lagged[:, part] = steps[lag : lag + window, :].astype(jnp.bfloat16)
    multiply(lagged, kernels, outs)


def correlate_again_kernel(lagged, kernels, after, *outs):
    multiply(lagged, kernels, outs)


def pair_kernel(mine, theirs, out):
    out[...] = (mine[...].astype(jnp.float32) + theirs[...].astype(jnp.float32)).astype(out.dtype)


def multiply(lagged, kernels, outs):
    unit = outs[0].shape[1]
    for low in (0, 2):
        product = jnp.dot(
            lagged[...],
            kernels[:, low * unit : low * unit + 2 * unit],
            preferred_element_type=jnp.float32,
        ).astype(jnp.bfloat16)
        outs[low][...] = product[:, :unit]
        outs[low + 1][...] = product[:, unit:]


def one_less_exp(y):
    series = jnp.ones_like(y)
    for k in range(9, 1, -1):
        series = 1.0 - series * y * (1.0 / k)
    return jnp.where(y < 0.5, y * series, 1.0 - jnp.exp(-y))


def factors_kernel(clocks, partner_clocks, near, far, rate, *refs):
    *outs, columns = refs
    chunks = len(outs)
    _, window, unit = outs[0].shape
    length = clocks.shape[1]
    rows = near.shape[1] - 128
    row, half = lax.axis_index("row"), lax.axis_index("tm") % 2
    first = pl.multiple_of(HALO + half * length, HALO)
    second = pl.multiple_of(HALO + (1 - half) * length, HALO)
    columns[0:HALO, :] = jnp.where(half == 1, far[:, rows : rows + 8], near[:, rows : rows + 8])
    columns[pl.ds(first, length), :] = clocks[...].T
    columns[pl.ds(second, length), :] = partner_clocks[...].T
    index = lax.broadcasted_iota(jnp.int32, (window, unit), 0) & 7
    for chunk, out in enumerate(outs):
        start = pl.multiple_of(((row * 2 + half) * chunks + chunk) * unit, unit)
        spent = columns[:, 0:1] * rate[:, pl.ds(start, unit)]
        out[0] = jnp.sqrt(one_less_exp(2.0 * spent))
        kept = jnp.exp(-spent) * columns[:, 1:2]
        for slot, shift in ((1, 1), (2, 2), (3, 4)):
            inside = index < 8 - shift
            out[slot] = jnp.where(inside, kept, 0.0)
            kept = jnp.where(inside, kept * pltpu.roll(kept, window - shift, 0), kept)
        out[4] = kept
        carry = jnp.ones((1, unit), jnp.float32)
        for group in range(window // 8 - 1, -1, -1):
            block = kept[group * 8 : group * 8 + 8] * carry
            out[5, group * 8 : group * 8 + 8, :] = block
            carry = block[0:1]


def recurrence_kernel(*refs):
    terms = refs[: 4 * CHUNKS]
    partials, first = refs[4 * CHUNKS : -1], refs[-1]
    for chunk in range(CHUNKS):
        own, direct, paired, factors = terms[4 * chunk : 4 * chunk + 4]
        window, unit = own.shape
        total = (
            own[...].astype(jnp.float32)
            + direct[...].astype(jnp.float32)
            + paired[...].astype(jnp.float32)
        )
        state = factors[0] * total
        for slot, shift in ((1, 1), (2, 2), (3, 4)):
            state = state + factors[slot] * pltpu.roll(state, window - shift, 0)
        carry = jnp.zeros((1, unit), jnp.float32)
        for group in range(window // 8 - 1, -1, -1):
            rows = slice(group * 8, group * 8 + 8)
            block = state[rows] + factors[4, rows, :] * carry
            partials[chunk][rows, :] = block
            carry = block[0:1]
            if group * 8 == HALO:
                first[chunk] = jnp.broadcast_to(carry, (8, unit))


def finish_kernel(incoming, admittance, *refs):
    given, (*outs, states) = refs[: 2 * CHUNKS], refs[2 * CHUNKS :]
    drives, mine, theirs = outs[:CHUNKS], outs[CHUNKS], outs[CHUNKS + 1]
    window, unit = states.shape
    length = mine.shape[1]
    row, half = lax.axis_index("row"), lax.axis_index("tm") % 2
    first = pl.multiple_of(HALO + half * length, HALO)
    second = pl.multiple_of(HALO + (1 - half) * length, HALO)
    for chunk in range(CHUNKS):
        partial, factors = given[2 * chunk : 2 * chunk + 2]
        start = pl.multiple_of(((row * 2 + half) * CHUNKS + chunk) * unit, unit)
        state = partial[...] + factors[5] * incoming[chunk, 0:1, :]
        drives[chunk][...] = (admittance[:, pl.ds(start, unit)] * state).astype(jnp.bfloat16)
        states[...] = state
        part = slice(chunk * unit, chunk * unit + unit)
        mine[part, :] = states[pl.ds(first, length), :].T
        theirs[part, :] = states[pl.ds(second, length), :].T


def reconstruct_kernel(last, d0, d1, d2, d3, kernels, *refs):
    if last:
        before, keep, send, total, steps, lagged = refs
    else:
        total, steps, lagged = refs
    lags, width, _ = lagged.shape
    unit = d0.shape[1]
    rows = total.shape[0]
    for slot, drive in enumerate((d0, d1, d2, d3)):
        steps[:, slot * unit : slot * unit + unit] = drive[...].astype(jnp.float32)
    for lag in range(lags):
        lagged[lag] = steps[HALO - lag : HALO - lag + width, :].astype(jnp.bfloat16)
    added = before[...] if last else None
    for lag in range(lags):
        term = lax.dot_general(
            kernels[lag * rows : lag * rows + rows, :],
            lagged[lag],
            (((1,), (1,)), ((), ())),
            preferred_element_type=jnp.float32,
        )
        added = term if added is None else added + term
    total[...] = added
    if last:
        length = width // 2
        half = lax.axis_index("tm") % 2
        keep[...] = total[:, pl.ds(pl.multiple_of(half * length, length), length)]
        send[...] = total[:, pl.ds(pl.multiple_of((1 - half) * length, length), length)].astype(
            send.dtype
        )


def call(kernel, name, in_specs, out_specs, out_shape, scratch, flops, moved):
    return pl.pallas_call(
        kernel,
        in_specs=in_specs,
        out_specs=out_specs,
        out_shape=out_shape,
        scratch_shapes=scratch,
        cost_estimate=pl.CostEstimate(flops=flops, bytes_accessed=moved, transcendentals=0),
        compiler_params=pltpu.CompilerParams(vmem_limit_bytes=VMEM_BYTES),
        name=name,
    )


def paired(
    traces,
    weights,
    pattern,
    cluster,
    element_damping_rate,
    local_step_length,
    housing_keep_share,
    admittance,
):
    rows, length = traces.shape
    lags = weights.shape[0]
    window = HALO + 2 * length
    unit = rows // (2 * CHUNKS)
    half = lax.axis_index("tm") % 2
    odd = half == 1
    f32, bf16 = jnp.float32, jnp.bfloat16
    tm_count = lax.axis_size("tm")
    swap = [(i, i ^ 1) for i in range(tm_count)]
    near = [(i, i + 1 if i % 2 else i - 1) for i in range(tm_count)]
    near = [(i, j) for i, j in near if 0 <= j < tm_count]
    far = [(i, i + 2 if i % 2 else i - 2) for i in range(tm_count)]
    far = [(i, j) for i, j in far if 0 <= j < tm_count]
    vmem = pl.BlockSpec(memory_space=pltpu.VMEM)

    hbm = pl.BlockSpec(memory_space=pltpu.HBM)
    barrier = lax.optimization_barrier

    def held(array):
        return pltpu.with_memory_space_constraint(array, pltpu.HBM)

    any_where = pl.BlockSpec(memory_space=pl.ANY)
    edge, clocks, columns, bits = call(
        setup_kernel,
        "setup",
        [hbm] * 5,
        [vmem] * 4,
        [
            jax.ShapeDtypeStruct((HALO, rows + 128), f32),
            jax.ShapeDtypeStruct((8, length), f32),
            jax.ShapeDtypeStruct((rows, 8), jnp.int32),
            jax.ShapeDtypeStruct((1, cluster.shape[0]), jnp.int32),
        ],
        [
            pltpu.VMEM((rows, length), bf16),
            pltpu.VMEM((length, rows + 128), f32),
            pltpu.VMEM(pattern.shape, jnp.int32),
            pltpu.VMEM((1, cluster.shape[0]), jnp.int32),
            pltpu.SemaphoreType.DMA((5,)),
        ],
        rows * length * 4,
        rows * length * 2,
    )(
        held(traces),
        held(local_step_length[None]),
        held(housing_keep_share[None]),
        held(pattern),
        held(cluster[None]),
    )
    partner_clocks = lax.ppermute(clocks, "tm", swap)
    own_traces, _ = barrier((traces, clocks))
    partner = lax.ppermute(own_traces, "tm", swap)
    got_near = lax.ppermute(edge, "tm", near)
    got_far = lax.ppermute(edge, "tm", far)

    strip = jax.ShapeDtypeStruct((window, unit), bf16)
    share_bytes = 4 * lags * rows * unit * 2
    share_flops = 2 * 4 * lags * rows * unit * window

    def chosen(chunk, columns):
        return call(
            functools.partial(mask_kernel, chunk),
            "mask",
            [vmem] * 2 + [hbm],
            vmem,
            pltpu.VMEM((lags * rows, 4 * unit), bf16),
            [pltpu.VMEM((rows, 128), jnp.int32), pltpu.SemaphoreType.DMA((4, lags))],
            share_bytes,
            share_bytes,
        )(columns, bits, weights)

    def correlated(kernels):
        *strips, lagged = call(
            correlate_kernel,
            "correlate",
            [hbm] * 2 + [vmem] * 3,
            [vmem] * 5,
            [strip] * 4 + [pltpu.VMEM((window, lags * rows), bf16)],
            [
                pltpu.VMEM((window + HALO, rows), f32),
                pltpu.VMEM((rows, length), bf16),
                pltpu.VMEM((rows, length), bf16),
                pltpu.SemaphoreType.DMA((2,)),
            ],
            share_flops,
            share_bytes // 2,
        )(held(traces), partner, got_near, got_far, kernels)
        return strips, lagged

    def correlated_again(lagged, kernels, after):
        return call(
            correlate_again_kernel,
            "correlate",
            [vmem] * 2 + [any_where],
            [vmem] * 4,
            [strip] * 4,
            [],
            share_flops,
            share_bytes // 2,
        )(lagged, kernels, after)

    def added(mine, theirs):
        return call(
            pair_kernel, "pair", [vmem] * 2, vmem, strip, [], window * unit, window * unit * 6
        )(mine, theirs)

    def over_row(array, by):
        return lax.ppermute(array, "row", [(i, i ^ by) for i in range(4)])

    def factored(clocks):
        return call(
            factors_kernel,
            "factors",
            [vmem] * 5,
            [vmem] * CHUNKS,
            [jax.ShapeDtypeStruct((6, window, unit), f32)] * CHUNKS,
            [pltpu.VMEM((window, 8), f32)],
            CHUNKS * window * unit * 100,
            CHUNKS * window * unit * 24,
        )(clocks, partner_clocks, got_near, got_far, element_damping_rate[None])

    def recurrence(parts, factors):
        given = [x for part, factor in zip(parts, factors) for x in (*part, factor)]
        *partials, first = call(
            recurrence_kernel,
            "recurrence",
            [vmem] * len(given),
            [vmem] * (CHUNKS + 1),
            [jax.ShapeDtypeStruct((window, unit), f32)] * CHUNKS
            + [jax.ShapeDtypeStruct((CHUNKS, 8, unit), f32)],
            [],
            CHUNKS * window * unit * 20,
            CHUNKS * window * unit * 30,
        )(*given)
        return partials, first

    def finished(partials, incoming, factors):
        given = [x for pair in zip(partials, factors) for x in pair]
        piece = jax.ShapeDtypeStruct((CHUNKS * unit, length), f32)
        *drives, mine, theirs = call(
            finish_kernel,
            "finish",
            [vmem] * (2 + len(given)),
            [vmem] * (CHUNKS + 2),
            [strip] * CHUNKS + [piece] * 2,
            [pltpu.VMEM((window, unit), f32)],
            CHUNKS * window * unit * 10,
            CHUNKS * window * unit * 16,
        )(incoming, admittance[None], *given)
        return drives, mine, theirs

    def reconstructed(drives, kernels, before):
        last = before is not None
        scratch = [
            pltpu.VMEM((window, 4 * unit), f32),
            pltpu.VMEM((lags, 2 * length, 4 * unit), bf16),
        ]
        out_shape = jax.ShapeDtypeStruct((rows, 2 * length), f32)
        if last:
            out_shape = [
                jax.ShapeDtypeStruct((rows, length), f32),
                jax.ShapeDtypeStruct((rows, length), bf16),
            ]
            scratch = [pltpu.VMEM((rows, 2 * length), f32)] + scratch
        return call(
            functools.partial(reconstruct_kernel, last),
            "reconstruct",
            [vmem] * (6 if last else 5),
            [vmem] * 2 if last else vmem,
            out_shape,
            scratch,
            share_flops,
            share_bytes // 2,
        )(*drives, kernels, *([before] if last else []))

    kernels = [chosen(0, columns)]
    strips_a, lagged = correlated(kernels[0])
    s3 = over_row(strips_a[3], 1)
    direct_a = over_row(strips_a[1], 1)
    late_columns, _ = barrier((columns, strips_a[0]))
    kernels.append(chosen(1, late_columns))
    pair_a = added(strips_a[2], s3)
    paired_a = over_row(pair_a, 2)
    strips_b = correlated_again(lagged, kernels[1], pair_a)
    pair_b = added(strips_b[2], over_row(strips_b[3], 1))
    paired_b = over_row(pair_b, 2)
    o1, _ = barrier((strips_b[1], pair_b))
    direct_b = over_row(o1, 1)
    parts = [(strips_a[0], direct_a, paired_a), (strips_b[0], direct_b, paired_b)]
    factors = factored(clocks)
    partials, first = recurrence(parts, factors)
    incoming = lax.ppermute(first, "tm", [(i, i - 2) for i in range(2, tm_count)])
    owned, mine, theirs = finished(partials, incoming, factors)
    theirs = lax.ppermute(theirs, "tm", swap)
    drives = []
    for drive in owned:
        d2 = over_row(drive, 2)
        drives.append((drive, over_row(drive, 1), d2, over_row(d2, 1)))
    total = None
    for chunk in range(CHUNKS):
        total = reconstructed(drives[chunk], kernels[chunk], total)
    keep, send = total
    pressure = keep + lax.ppermute(send, "tm", swap).astype(f32)
    state = jnp.where(
        odd, jnp.concatenate([theirs, mine], 0), jnp.concatenate([mine, theirs], 0)
    )
    return (state, pressure.astype(bf16))


def local(traces, weights, pattern, *rest):
    rows, length = traces.shape
    fits = (
        lax.axis_size("row") == 4
        and lax.axis_size("tm") == 4
        and length == 128
        and rows % (256 * CHUNKS) == 0
        and weights.shape[0] <= 8
        and pattern.shape[1] <= 32
    )
    return (paired if fits else general)(traces, weights, pattern, *rest)


def solution(mesh):
    placed = (P("row", ("group", "tm")), P(None, "row", None), P(), P(), P(), P("tm"), P("tm"), P())
    return jax.shard_map(
        local,
        mesh=mesh,
        in_specs=placed,
        out_specs=(P("row", ("group", "tm")), P("row", ("group", "tm"))),
        check_vma=False,
    )
```

```python
import functools

import jax
import jax.numpy as jnp
from jax import lax
from jax.experimental import pallas as pl
from jax.experimental.pallas import tpu as pltpu
from jax.sharding import PartitionSpec as P

HALO = 16
VMEM_BYTES = 20 << 20


def carried_in(array, axis, join, neutral):
    count = lax.axis_size(axis)
    place = lax.axis_index(axis)
    ahead = count - 1 - place
    gathered = jax.tree.map(
        lambda a, kind: lax.all_gather(a.astype(kind), axis),
        array,
        jax.tree.map(lambda a: jnp.bfloat16 if a.dtype == jnp.float32 else a.dtype, array),
    )
    state = jax.tree.map(lambda a, e: jnp.zeros_like(a) + jnp.asarray(e, a.dtype), array, neutral)

    def one(hop, state):
        source = count - 1 - hop
        return join(
            state,
            jax.tree.map(
                lambda a, own: lax.dynamic_index_in_dim(a, source, 0, False).astype(own.dtype),
                gathered,
                array,
            ),
        )

    return lax.fori_loop(0, ahead, one, state)


def from_behind(array, axis, by):
    count = lax.axis_size(axis)
    pairs = [(i, i + by) for i in range(count) if 0 <= i + by < count]
    return lax.ppermute(array, axis, pairs)


def lag_kernels(weights, pattern, cluster, first_row):
    local_rows = weights.shape[1]
    own_labels = lax.dynamic_slice_in_dim(cluster, first_row, local_rows, 0)
    labels = jnp.arange(pattern.shape[1], dtype=jnp.int32)
    row_onehot = (own_labels[:, None] == labels[None, :]).astype(jnp.bfloat16)
    column_onehot = (labels[:, None] == cluster[None, :]).astype(jnp.bfloat16)
    kernels = []
    for lag_index in range(weights.shape[0]):
        picked = jnp.dot(
            row_onehot, pattern[lag_index].astype(jnp.bfloat16), preferred_element_type=jnp.float32
        )
        table = jnp.dot(
            picked.astype(jnp.bfloat16), column_onehot, preferred_element_type=jnp.float32
        )
        kernels.append(weights[lag_index] * table.astype(jnp.bfloat16))
    return kernels


def correlate(kernels, extended):
    length = extended.shape[1] - len(kernels) + 1
    running = None
    for lag_index in range(len(kernels)):
        product_term = lax.dot_general(
            kernels[lag_index],
            extended[:, lag_index : lag_index + length],
            (((0,), (0,)), ((), ())),
            preferred_element_type=jnp.float32,
        )
        running = product_term if running is None else running + product_term
    return running


def reconstruct(kernels, extended):
    number_of_lags = len(kernels)
    length = extended.shape[1] - number_of_lags + 1
    running = None
    for lag_index in range(number_of_lags):
        offset = number_of_lags - 1 - lag_index
        product_term = jnp.dot(
            kernels[lag_index],
            extended[:, offset : offset + length],
            preferred_element_type=jnp.float32,
        )
        running = product_term if running is None else running + product_term
    return running


def chain_step(earlier, later):
    return (later[0] * earlier[0], later[1] + later[0] * earlier[1])


def block_recurrence(keep_fraction, inflow):
    def advance(carry, pieces):
        kept_now, state_now = carry
        keep, more = pieces
        state_now = keep * state_now + more
        kept_now = keep * kept_now
        return ((kept_now, state_now), (kept_now, state_now))

    elements = keep_fraction.shape[0]
    start = (jnp.ones((elements,), jnp.float32), jnp.zeros((elements,), jnp.float32))
    _, outputs = lax.scan(advance, start, (keep_fraction.T, inflow.T), reverse=True)
    return (outputs[0].T, outputs[1].T)


def general(
    traces,
    weights,
    pattern,
    cluster,
    element_damping_rate,
    local_step_length,
    housing_keep_share,
    admittance,
):
    local_rows = traces.shape[0]
    length = traces.shape[1]
    number_of_lags = weights.shape[0]
    first_row = lax.axis_index("row") * local_rows
    kernels = lag_kernels(weights, pattern, cluster, first_row)
    trailing = from_behind(traces[:, : number_of_lags - 1], "tm", -1)
    extended = jnp.concatenate([traces, trailing], 1)
    adjoint_sum = lax.psum(correlate(kernels, extended).astype(jnp.bfloat16), "row").astype(
        jnp.float32
    )
    spent = element_damping_rate[:, None] * local_step_length[None, :]
    keep_fraction = jnp.exp(-spent) * housing_keep_share[None, :]
    inflow = jnp.sqrt(-jnp.expm1(-2.0 * spent)) * adjoint_sum
    retained, partial_state = block_recurrence(keep_fraction, inflow)
    neutral = (jnp.ones_like(retained[:, 0]), jnp.zeros_like(partial_state[:, 0]))
    incoming = carried_in((retained[:, 0], partial_state[:, 0]), "tm", chain_step, neutral)
    state = partial_state + retained * incoming[1][:, None]
    driving = (admittance[:, None] * state).astype(jnp.bfloat16)
    leading = from_behind(driving[:, length - number_of_lags + 1 :], "tm", 1)
    pressure = reconstruct(kernels, jnp.concatenate([leading, driving], 1))
    state = lax.dynamic_slice_in_dim(state, first_row, local_rows, 0)
    return (state, pressure.astype(jnp.bfloat16))


def setup_kernel(
    traces_in,
    length_in,
    share_in,
    pattern_in,
    cluster_in,
    edge,
    clocks,
    columns,
    bits,
    own,
    traces,
    turned,
    pattern,
    cluster,
    ready,
):
    rows, length = traces.shape
    lags, kinds, _ = pattern.shape
    row, odd = lax.axis_index("row"), lax.axis_index("tm") % 2
    moves = (
        (traces_in, traces),
        (length_in, clocks.at[0:1, :]),
        (share_in, clocks.at[1:2, :]),
        (pattern_in, pattern),
        (cluster_in, cluster),
    )
    clocks[...] = jnp.zeros_like(clocks)
    copies = [
        pltpu.make_async_copy(source, target, ready.at[index])
        for index, (source, target) in enumerate(moves)
    ]
    for copy in copies:
        copy.start()
    for copy in copies:
        copy.wait()
    turned[:, 0:rows] = traces[...].astype(jnp.float32).T
    turned[:, rows:] = jnp.zeros((length, 128), jnp.float32)
    turned[:, rows : rows + 8] = clocks[...].T
    edge[...] = turned[pl.ds(pl.multiple_of(odd * (length - HALO), HALO), HALO), :]
    own[...] = turned[:, 0:rows].astype(jnp.bfloat16)

    bits[...] = jnp.int32(1) << cluster[...]
    labels = cluster[:, pl.ds(pl.multiple_of(row * rows, rows), rows)]
    hit = lax.broadcasted_iota(jnp.int32, (kinds, rows), 0) == labels
    places = lax.broadcasted_iota(jnp.int32, (kinds, pattern.shape[2]), 1)
    found = []
    for lag in range(lags):
        word = (pattern[lag] << places).sum(1, keepdims=True)
        found.append(jnp.where(hit, word, 0).sum(0, keepdims=True))
    found = jnp.concatenate(found + [jnp.zeros((8 - lags, rows), jnp.int32)], 0)
    columns[...] = found.T


def mask_kernel(slots, columns, bits, weights, kernels, spread, arrived):
    lags, rows, _ = weights.shape
    unit = kernels.shape[1] // len(slots)
    row, half = lax.axis_index("row"), lax.axis_index("tm") % 2

    def start_of(slot):
        return pl.multiple_of((jnp.bitwise_xor(row, slot) * 2 + half) * unit, unit)

    def fetch(lag, index):
        return pltpu.make_async_copy(
            weights.at[lag, :, pl.ds(start_of(slots[index]), unit)],
            kernels.at[pl.ds(lag * rows, rows), pl.ds(index * unit, unit)],
            arrived.at[index, lag],
        )

    blocks = [(lag, index) for lag in range(lags) for index in range(len(slots))]
    for block in blocks:
        fetch(*block).start()
    picked = [bits[:, pl.ds(start_of(slot), unit)] for slot in slots]
    for lag, index in blocks:
        if index == 0:
            spread[...] = jnp.broadcast_to(columns[:, lag : lag + 1], (rows, 128))
        fetch(lag, index).wait()
        for at in range(0, unit, 128):
            place = slice(lag * rows, lag * rows + rows)
            part = slice(index * unit + at, index * unit + at + 128)
            weight = kernels[place, part]
            keep = (spread[...] & picked[index][:, at : at + 128]) != 0
            kernels[place, part] = jnp.where(keep, weight, jnp.zeros_like(weight))


def correlate_kernel(own, partner, near, far, kernels, *refs):
    *outs, lagged, steps = refs
    length, rows = own.shape
    window = lagged.shape[0]
    lags = lagged.shape[1] // rows
    half = lax.axis_index("tm") % 2
    odd = half == 1
    first = pl.multiple_of(HALO + half * length, HALO)
    second = pl.multiple_of(HALO + (1 - half) * length, HALO)
    steps[0:HALO, :] = jnp.where(odd, far[:, 0:rows], near[:, 0:rows])
    steps[window : window + HALO, :] = jnp.where(odd, near[:, 0:rows], far[:, 0:rows])
    steps[pl.ds(first, length), :] = own[...].astype(jnp.float32)
    steps[pl.ds(second, length), :] = partner[...].astype(jnp.float32)
    for lag in range(lags):
        part = slice(lag * rows, lag * rows + rows)
        lagged[:, part] = steps[lag : lag + window, :].astype(jnp.bfloat16)
    multiply(lagged, kernels, outs)


def correlate_again_kernel(lagged, kernels, *outs):
    multiply(lagged, kernels, outs)


def multiply(lagged, kernels, outs):
    unit = outs[0].shape[1]
    for index, out in enumerate(outs):
        out[...] = jnp.dot(
            lagged[...],
            kernels[:, index * unit : index * unit + unit],
            preferred_element_type=jnp.float32,
        ).astype(out.dtype)


def pair_kernel(mine, theirs, out):
    out[...] = (mine[...].astype(jnp.float32) + theirs[...].astype(jnp.float32)).astype(out.dtype)


def one_less_exp(y):
    series = jnp.ones_like(y)
    for k in range(9, 1, -1):
        series = 1.0 - series * y * (1.0 / k)
    return jnp.where(y < 0.5, y * series, 1.0 - jnp.exp(-y))


def factors_kernel(clocks, partner_clocks, near, far, rate, out, columns):
    _, window, unit = out.shape
    length = clocks.shape[1]
    rows = near.shape[1] - 128
    row, half = lax.axis_index("row"), lax.axis_index("tm") % 2
    first = pl.multiple_of(HALO + half * length, HALO)
    second = pl.multiple_of(HALO + (1 - half) * length, HALO)
    columns[0:HALO, :] = jnp.where(half == 1, far[:, rows : rows + 8], near[:, rows : rows + 8])
    columns[pl.ds(first, length), :] = clocks[...].T
    columns[pl.ds(second, length), :] = partner_clocks[...].T
    index = lax.broadcasted_iota(jnp.int32, (window, unit), 0) & 7
    start = pl.multiple_of((row * 2 + half) * unit, unit)
    spent = columns[:, 0:1] * rate[:, pl.ds(start, unit)]
    out[0] = jnp.sqrt(one_less_exp(2.0 * spent))
    kept = jnp.exp(-spent) * columns[:, 1:2]
    for slot, shift in ((1, 1), (2, 2), (3, 4)):
        inside = index < 8 - shift
        out[slot] = jnp.where(inside, kept, 0.0)
        kept = jnp.where(inside, kept * pltpu.roll(kept, window - shift, 0), kept)
    out[4] = kept
    carry = jnp.ones((1, unit), jnp.float32)
    for group in range(window // 8 - 1, -1, -1):
        block = kept[group * 8 : group * 8 + 8] * carry
        out[5, group * 8 : group * 8 + 8, :] = block
        carry = block[0:1]


def recurrence_kernel(own, direct, paired, factors, partial, first):
    window, unit = own.shape
    total = (
        own[...].astype(jnp.float32)
        + direct[...].astype(jnp.float32)
        + paired[...].astype(jnp.float32)
    )
    state = factors[0] * total
    for slot, shift in ((1, 1), (2, 2), (3, 4)):
        state = state + factors[slot] * pltpu.roll(state, window - shift, 0)
    carry = jnp.zeros((1, unit), jnp.float32)
    for group in range(window // 8 - 1, -1, -1):
        rows = slice(group * 8, group * 8 + 8)
        block = state[rows] + factors[4, rows, :] * carry
        partial[rows, :] = block
        carry = block[0:1]
        if group * 8 == HALO:
            first[...] = jnp.broadcast_to(carry, first.shape)


def finish_kernel(incoming, admittance, partial, factors, drive, mine, theirs, states):
    window, unit = states.shape
    length = mine.shape[1]
    row, half = lax.axis_index("row"), lax.axis_index("tm") % 2
    first = pl.multiple_of(HALO + half * length, HALO)
    second = pl.multiple_of(HALO + (1 - half) * length, HALO)
    start = pl.multiple_of((row * 2 + half) * unit, unit)
    state = partial[...] + factors[5] * incoming[0:1, :]
    drive[...] = (admittance[:, pl.ds(start, unit)] * state).astype(jnp.bfloat16)
    states[...] = state
    mine[...] = states[pl.ds(first, length), :].T
    theirs[...] = states[pl.ds(second, length), :].T


def reconstruct_kernel(count, at, stage, *refs):
    drives, (kernels, *refs) = refs[:count], refs[count:]
    if stage == "last":
        before, keep, send, steps, lagged = refs
    elif stage == "next":
        before, total, steps, lagged = refs
    else:
        total, steps, lagged = refs
    lags, width, _ = lagged.shape
    unit = drives[0].shape[1]
    rows = kernels.shape[0] // lags
    for slot, drive in enumerate(drives):
        steps[:, slot * unit : slot * unit + unit] = drive[...].astype(jnp.float32)
    for lag in range(lags):
        lagged[lag] = steps[HALO - lag : HALO - lag + width, :].astype(jnp.bfloat16)
    added = None if stage == "first" else before[...]
    for lag in range(lags):
        term = lax.dot_general(
            kernels[lag * rows : lag * rows + rows, at * unit : (at + count) * unit],
            lagged[lag],
            (((1,), (1,)), ((), ())),
            preferred_element_type=jnp.float32,
        )
        added = term if added is None else added + term
    if stage == "last":
        length = width // 2
        odd = lax.axis_index("tm") % 2 == 1
        keep[...] = jnp.where(odd, added[:, length:], added[:, :length])
        send[...] = jnp.where(odd, added[:, :length], added[:, length:]).astype(send.dtype)
    else:
        total[...] = added


def call(kernel, name, in_specs, out_specs, out_shape, scratch, flops, moved):
    return pl.pallas_call(
        kernel,
        in_specs=in_specs,
        out_specs=out_specs,
        out_shape=out_shape,
        scratch_shapes=scratch,
        cost_estimate=pl.CostEstimate(flops=flops, bytes_accessed=moved, transcendentals=0),
        compiler_params=pltpu.CompilerParams(vmem_limit_bytes=VMEM_BYTES),
        name=name,
    )


def paired(
    traces,
    weights,
    pattern,
    cluster,
    element_damping_rate,
    local_step_length,
    housing_keep_share,
    admittance,
):
    rows, length = traces.shape
    lags = weights.shape[0]
    window = HALO + 2 * length
    unit = rows // 2
    half = lax.axis_index("tm") % 2
    odd = half == 1
    f32, bf16 = jnp.float32, jnp.bfloat16
    tm_count = lax.axis_size("tm")
    swap = [(i, i ^ 1) for i in range(tm_count)]
    near = [(i, i + 1 if i % 2 else i - 1) for i in range(tm_count)]
    near = [(i, j) for i, j in near if 0 <= j < tm_count]
    far = [(i, i + 2 if i % 2 else i - 2) for i in range(tm_count)]
    far = [(i, j) for i, j in far if 0 <= j < tm_count]
    vmem = pl.BlockSpec(memory_space=pltpu.VMEM)

    hbm = pl.BlockSpec(memory_space=pltpu.HBM)
    barrier = lax.optimization_barrier

    def held(array):
        return pltpu.with_memory_space_constraint(array, pltpu.HBM)

    edge, clocks, columns, bits, own = call(
        setup_kernel,
        "setup",
        [hbm] * 5,
        [vmem] * 5,
        [
            jax.ShapeDtypeStruct((HALO, rows + 128), f32),
            jax.ShapeDtypeStruct((8, length), f32),
            jax.ShapeDtypeStruct((rows, 8), jnp.int32),
            jax.ShapeDtypeStruct((1, cluster.shape[0]), jnp.int32),
            jax.ShapeDtypeStruct((length, rows), bf16),
        ],
        [
            pltpu.VMEM((rows, length), bf16),
            pltpu.VMEM((length, rows + 128), f32),
            pltpu.VMEM(pattern.shape, jnp.int32),
            pltpu.VMEM((1, cluster.shape[0]), jnp.int32),
            pltpu.SemaphoreType.DMA((5,)),
        ],
        rows * length * 4,
        rows * length * 2,
    )(
        held(traces),
        held(local_step_length[None]),
        held(housing_keep_share[None]),
        held(pattern),
        held(cluster[None]),
    )
    partner_clocks = lax.ppermute(clocks, "tm", swap)
    partner = lax.ppermute(own, "tm", swap)
    got_near = lax.ppermute(edge, "tm", near)
    got_far = lax.ppermute(edge, "tm", far)

    strip = jax.ShapeDtypeStruct((window, unit), bf16)
    share_bytes = 2 * lags * rows * unit * 2
    share_flops = 2 * 2 * lags * rows * unit * window

    def chosen(slots, columns):
        return call(
            functools.partial(mask_kernel, slots),
            "mask",
            [vmem] * 2 + [hbm],
            vmem,
            pltpu.VMEM((lags * rows, len(slots) * unit), bf16),
            [pltpu.VMEM((rows, 128), jnp.int32), pltpu.SemaphoreType.DMA((len(slots), lags))],
            share_bytes,
            share_bytes,
        )(columns, bits, weights)

    def correlated(kernels):
        return call(
            correlate_kernel,
            "correlate",
            [vmem] * 5,
            [vmem] * 3,
            [strip] * 2 + [pltpu.VMEM((window, lags * rows), bf16)],
            [pltpu.VMEM((window + HALO, rows), f32)],
            share_flops,
            share_bytes // 2,
        )(own, partner, got_near, got_far, kernels)

    def correlated_again(lagged, kernels):
        return call(
            correlate_again_kernel,
            "correlate",
            [vmem] * 2,
            [vmem] * 2,
            [strip] * 2,
            [],
            share_flops,
            share_bytes // 2,
        )(lagged, kernels)

    def added(mine, theirs):
        return call(
            pair_kernel, "pair", [vmem] * 2, vmem, strip, [], window * unit, window * unit * 6
        )(mine, theirs)

    def over_row(array, by):
        return lax.ppermute(array, "row", [(i, i ^ by) for i in range(4)])

    def factored(clocks):
        return call(
            factors_kernel,
            "factors",
            [vmem] * 5,
            vmem,
            jax.ShapeDtypeStruct((6, window, unit), f32),
            [pltpu.VMEM((window, 8), f32)],
            window * unit * 100,
            window * unit * 24,
        )(clocks, partner_clocks, got_near, got_far, element_damping_rate[None])

    def recurrence(terms, factors):
        return call(
            recurrence_kernel,
            "recurrence",
            [vmem] * 4,
            [vmem] * 2,
            [jax.ShapeDtypeStruct((window, unit), f32), jax.ShapeDtypeStruct((8, unit), f32)],
            [],
            window * unit * 20,
            window * unit * 30,
        )(*terms, factors)

    def finished(partial, incoming, factors):
        piece = jax.ShapeDtypeStruct((unit, length), f32)
        return call(
            finish_kernel,
            "finish",
            [vmem] * 4,
            [vmem] * 3,
            [strip, piece, piece],
            [pltpu.VMEM((window, unit), f32)],
            window * unit * 10,
            window * unit * 16,
        )(incoming, admittance[None], partial, factors)

    def reconstructed(stage, at, drives, kernels, *before):
        count = len(drives)
        out_shape = jax.ShapeDtypeStruct((rows, 2 * length), f32)
        if stage == "last":
            out_shape = [
                jax.ShapeDtypeStruct((rows, length), f32),
                jax.ShapeDtypeStruct((rows, length), bf16),
            ]
        return call(
            functools.partial(reconstruct_kernel, count, at, stage),
            "reconstruct",
            [vmem] * (count + 1 + len(before)),
            [vmem] * 2 if stage == "last" else vmem,
            out_shape,
            [
                pltpu.VMEM((window, count * unit), f32),
                pltpu.VMEM((lags, 2 * length, count * unit), bf16),
            ],
            share_flops * count // 2,
            share_bytes * count // 4,
        )(*drives, kernels, *before)

    far_kernels = chosen((2, 3), columns)
    o2, o3, lagged = correlated(far_kernels)
    s3 = over_row(o3, 1)
    late_columns, _ = barrier((columns, o2))
    near_kernels = chosen((0, 1), late_columns)
    o0, o1 = correlated_again(lagged, near_kernels)
    paired = over_row(added(o2, s3), 2)
    direct = over_row(o1, 1)
    factors = factored(clocks)
    partial, first = recurrence((o0, direct, paired), factors)
    incoming = lax.ppermute(first, "tm", [(i, i - 2) for i in range(2, tm_count)])
    drive, mine, theirs = finished(partial, incoming, factors)
    d2 = over_row(drive, 2)
    d1 = over_row(drive, 1)
    d3 = over_row(d2, 1)
    theirs = lax.ppermute(theirs, "tm", swap)
    total = reconstructed("first", 0, (drive, d1), near_kernels)
    total = reconstructed("next", 0, (d2,), far_kernels, total)
    keep, send = reconstructed("last", 1, (d3,), far_kernels, total)
    pressure = keep + lax.ppermute(send, "tm", swap).astype(f32)
    state = jnp.where(
        odd, jnp.concatenate([theirs, mine], 0), jnp.concatenate([mine, theirs], 0)
    )
    return (state, pressure.astype(bf16))


def local(traces, weights, pattern, *rest):
    rows, length = traces.shape
    fits = (
        lax.axis_size("row") == 4
        and lax.axis_size("tm") == 4
        and length == 128
        and rows % 256 == 0
        and weights.shape[0] <= 8
        and pattern.shape[1] <= 32
    )
    return (paired if fits else general)(traces, weights, pattern, *rest)


def solution(mesh):
    placed = (P("row", ("group", "tm")), P(None, "row", None), P(), P(), P(), P("tm"), P("tm"), P())
    return jax.shard_map(
        local,
        mesh=mesh,
        in_specs=placed,
        out_specs=(P("row", ("group", "tm")), P("row", ("group", "tm"))),
        check_vma=False,
    )
```

```python
import functools

import jax
import jax.numpy as jnp
from jax import lax
from jax.experimental import pallas as pl
from jax.experimental.pallas import tpu as pltpu
from jax.sharding import PartitionSpec as P

HALO = 8
VMEM_BYTES = 20 << 20


def carried_in(array, axis, join, neutral):
    count = lax.axis_size(axis)
    place = lax.axis_index(axis)
    ahead = count - 1 - place
    gathered = jax.tree.map(
        lambda a, kind: lax.all_gather(a.astype(kind), axis),
        array,
        jax.tree.map(lambda a: jnp.bfloat16 if a.dtype == jnp.float32 else a.dtype, array),
    )
    state = jax.tree.map(lambda a, e: jnp.zeros_like(a) + jnp.asarray(e, a.dtype), array, neutral)

    def one(hop, state):
        source = count - 1 - hop
        return join(
            state,
            jax.tree.map(
                lambda a, own: lax.dynamic_index_in_dim(a, source, 0, False).astype(own.dtype),
                gathered,
                array,
            ),
        )

    return lax.fori_loop(0, ahead, one, state)


def from_behind(array, axis, by):
    count = lax.axis_size(axis)
    pairs = [(i, i + by) for i in range(count) if 0 <= i + by < count]
    return lax.ppermute(array, axis, pairs)


def lag_kernels(weights, pattern, cluster, first_row):
    local_rows = weights.shape[1]
    own_labels = lax.dynamic_slice_in_dim(cluster, first_row, local_rows, 0)
    labels = jnp.arange(pattern.shape[1], dtype=jnp.int32)
    row_onehot = (own_labels[:, None] == labels[None, :]).astype(jnp.bfloat16)
    column_onehot = (labels[:, None] == cluster[None, :]).astype(jnp.bfloat16)
    kernels = []
    for lag_index in range(weights.shape[0]):
        picked = jnp.dot(
            row_onehot, pattern[lag_index].astype(jnp.bfloat16), preferred_element_type=jnp.float32
        )
        table = jnp.dot(
            picked.astype(jnp.bfloat16), column_onehot, preferred_element_type=jnp.float32
        )
        kernels.append(weights[lag_index] * table.astype(jnp.bfloat16))
    return kernels


def correlate(kernels, extended):
    length = extended.shape[1] - len(kernels) + 1
    running = None
    for lag_index in range(len(kernels)):
        product_term = lax.dot_general(
            kernels[lag_index],
            extended[:, lag_index : lag_index + length],
            (((0,), (0,)), ((), ())),
            preferred_element_type=jnp.float32,
        )
        running = product_term if running is None else running + product_term
    return running


def reconstruct(kernels, extended):
    number_of_lags = len(kernels)
    length = extended.shape[1] - number_of_lags + 1
    running = None
    for lag_index in range(number_of_lags):
        offset = number_of_lags - 1 - lag_index
        product_term = jnp.dot(
            kernels[lag_index],
            extended[:, offset : offset + length],
            preferred_element_type=jnp.float32,
        )
        running = product_term if running is None else running + product_term
    return running


def chain_step(earlier, later):
    return (later[0] * earlier[0], later[1] + later[0] * earlier[1])


def block_recurrence(keep_fraction, inflow):
    def advance(carry, pieces):
        kept_now, state_now = carry
        keep, more = pieces
        state_now = keep * state_now + more
        kept_now = keep * kept_now
        return ((kept_now, state_now), (kept_now, state_now))

    elements = keep_fraction.shape[0]
    start = (jnp.ones((elements,), jnp.float32), jnp.zeros((elements,), jnp.float32))
    _, outputs = lax.scan(advance, start, (keep_fraction.T, inflow.T), reverse=True)
    return (outputs[0].T, outputs[1].T)


def general(
    traces,
    weights,
    pattern,
    cluster,
    element_damping_rate,
    local_step_length,
    housing_keep_share,
    admittance,
):
    local_rows = traces.shape[0]
    length = traces.shape[1]
    number_of_lags = weights.shape[0]
    first_row = lax.axis_index("row") * local_rows
    kernels = lag_kernels(weights, pattern, cluster, first_row)
    trailing = from_behind(traces[:, : number_of_lags - 1], "tm", -1)
    extended = jnp.concatenate([traces, trailing], 1)
    adjoint_sum = lax.psum(correlate(kernels, extended).astype(jnp.bfloat16), "row").astype(
        jnp.float32
    )
    spent = element_damping_rate[:, None] * local_step_length[None, :]
    keep_fraction = jnp.exp(-spent) * housing_keep_share[None, :]
    inflow = jnp.sqrt(-jnp.expm1(-2.0 * spent)) * adjoint_sum
    retained, partial_state = block_recurrence(keep_fraction, inflow)
    neutral = (jnp.ones_like(retained[:, 0]), jnp.zeros_like(partial_state[:, 0]))
    incoming = carried_in((retained[:, 0], partial_state[:, 0]), "tm", chain_step, neutral)
    state = partial_state + retained * incoming[1][:, None]
    driving = (admittance[:, None] * state).astype(jnp.bfloat16)
    leading = from_behind(driving[:, length - number_of_lags + 1 :], "tm", 1)
    pressure = reconstruct(kernels, jnp.concatenate([leading, driving], 1))
    state = lax.dynamic_slice_in_dim(state, first_row, local_rows, 0)
    return (state, pressure.astype(jnp.bfloat16))


def setup_kernel(
    traces_in,
    length_in,
    share_in,
    pattern_in,
    cluster_in,
    edge,
    clocks,
    columns,
    bits,
    own,
    traces,
    turned,
    pattern,
    cluster,
    ready,
):
    rows, length = traces.shape
    lags, kinds, _ = pattern.shape
    row, odd = lax.axis_index("row"), lax.axis_index("tm") % 2
    moves = (
        (traces_in, traces),
        (length_in, clocks.at[0:1, :]),
        (share_in, clocks.at[1:2, :]),
        (pattern_in, pattern),
        (cluster_in, cluster),
    )
    clocks[...] = jnp.zeros_like(clocks)
    copies = [
        pltpu.make_async_copy(source, target, ready.at[index])
        for index, (source, target) in enumerate(moves)
    ]
    for copy in copies:
        copy.start()
    for copy in copies:
        copy.wait()
    turned[:, 0:rows] = traces[...].astype(jnp.float32).T
    turned[:, rows:] = jnp.zeros((length, 128), jnp.float32)
    turned[:, rows : rows + 8] = clocks[...].T
    edge[...] = turned[pl.ds(pl.multiple_of(odd * (length - HALO), HALO), HALO), :]
    own[...] = turned[:, 0:rows].astype(jnp.bfloat16)

    bits[...] = jnp.int32(1) << cluster[...]
    labels = cluster[:, pl.ds(pl.multiple_of(row * rows, rows), rows)]
    hit = lax.broadcasted_iota(jnp.int32, (kinds, rows), 0) == labels
    places = lax.broadcasted_iota(jnp.int32, (kinds, pattern.shape[2]), 1)
    found = []
    for lag in range(lags):
        word = (pattern[lag] << places).sum(1, keepdims=True)
        found.append(jnp.where(hit, word, 0).sum(0, keepdims=True))
    found = jnp.concatenate(found + [jnp.zeros((8 - lags, rows), jnp.int32)], 0)
    columns[...] = found.T


def mask_kernel(slots, columns, bits, weights, kernels, spread, arrived):
    lags, rows, _ = weights.shape
    unit = kernels.shape[1] // len(slots)
    row, half = lax.axis_index("row"), lax.axis_index("tm") % 2

    def start_of(slot):
        return pl.multiple_of((jnp.bitwise_xor(row, slot) * 2 + half) * unit, unit)

    def fetch(lag, index):
        return pltpu.make_async_copy(
            weights.at[lag, :, pl.ds(start_of(slots[index]), unit)],
            kernels.at[pl.ds(lag * rows, rows), pl.ds(index * unit, unit)],
            arrived.at[index, lag],
        )

    blocks = [(lag, index) for lag in range(lags) for index in range(len(slots))]
    for block in blocks:
        fetch(*block).start()
    picked = [bits[:, pl.ds(start_of(slot), unit)] for slot in slots]
    for lag, index in blocks:
        if index == 0:
            spread[...] = jnp.broadcast_to(columns[:, lag : lag + 1], (rows, 128))
        fetch(lag, index).wait()
        for at in range(0, unit, 128):
            place = slice(lag * rows, lag * rows + rows)
            part = slice(index * unit + at, index * unit + at + 128)
            weight = kernels[place, part]
            keep = (spread[...] & picked[index][:, at : at + 128]) != 0
            kernels[place, part] = jnp.where(keep, weight, jnp.zeros_like(weight))


def correlate_kernel(own, partner, near, far, kernels, *refs):
    *outs, lagged, steps = refs
    length, rows = own.shape
    window = lagged.shape[0]
    lags = lagged.shape[1] // rows
    half = lax.axis_index("tm") % 2
    odd = half == 1
    first = pl.multiple_of(HALO + half * length, HALO)
    second = pl.multiple_of(HALO + (1 - half) * length, HALO)
    steps[0:HALO, :] = jnp.where(odd, far[:, 0:rows], near[:, 0:rows])
    steps[window : window + HALO, :] = jnp.where(odd, near[:, 0:rows], far[:, 0:rows])
    steps[pl.ds(first, length), :] = own[...].astype(jnp.float32)
    steps[pl.ds(second, length), :] = partner[...].astype(jnp.float32)
    for lag in range(lags):
        part = slice(lag * rows, lag * rows + rows)
        lagged[:, part] = steps[lag : lag + window, :].astype(jnp.bfloat16)
    multiply(lagged, kernels, outs)


def correlate_again_kernel(lagged, kernels, *outs):
    multiply(lagged, kernels, outs)


def multiply(lagged, kernels, outs):
    unit = outs[0].shape[1]
    for index, out in enumerate(outs):
        out[...] = jnp.dot(
            lagged[...],
            kernels[:, index * unit : index * unit + unit],
            preferred_element_type=jnp.float32,
        ).astype(out.dtype)


def pair_kernel(mine, theirs, out):
    out[...] = (mine[...].astype(jnp.float32) + theirs[...].astype(jnp.float32)).astype(out.dtype)


def one_less_exp(y):
    series = jnp.ones_like(y)
    for k in range(9, 1, -1):
        series = 1.0 - series * y * (1.0 / k)
    return jnp.where(y < 0.5, y * series, 1.0 - jnp.exp(-y))


def factors_kernel(
    clocks, partner_clocks, near, far, rate, admittance, out, reach, driven, columns
):
    _, window, unit = out.shape
    length = clocks.shape[1]
    rows = near.shape[1] - 128
    row, half = lax.axis_index("row"), lax.axis_index("tm") % 2
    first = pl.multiple_of(HALO + half * length, HALO)
    second = pl.multiple_of(HALO + (1 - half) * length, HALO)
    columns[0:HALO, :] = jnp.where(half == 1, far[:, rows : rows + 8], near[:, rows : rows + 8])
    columns[pl.ds(first, length), :] = clocks[...].T
    columns[pl.ds(second, length), :] = partner_clocks[...].T

    def part_of(array, slot):
        start = pl.multiple_of((jnp.bitwise_xor(row, slot) * 2 + half) * unit, unit)
        return array[:, pl.ds(start, unit)]

    index = lax.broadcasted_iota(jnp.int32, (window, unit), 0) & 7
    spent = columns[:, 0:1] * part_of(rate, 0)
    out[0] = jnp.sqrt(one_less_exp(2.0 * spent))
    kept = jnp.exp(-spent) * columns[:, 1:2]
    for slot, shift in ((1, 1), (2, 2), (3, 4)):
        inside = index < 8 - shift
        out[slot] = jnp.where(inside, kept, 0.0)
        kept = jnp.where(inside, kept * pltpu.roll(kept, window - shift, 0), kept)
    out[4] = kept

    spans = jnp.broadcast_to(columns[:, 0:1], (window, 128))
    shares = jnp.broadcast_to(columns[:, 1:2], (window, 128))
    inside = index[:, 0:128]
    for shift in (1, 2, 4):
        later = pltpu.roll(spans, window - shift, 0)
        spans = jnp.where(inside < 8 - shift, spans + later, spans)
        later = pltpu.roll(shares, window - shift, 0)
        shares = jnp.where(inside < 8 - shift, shares * later, shares)
    span, share = jnp.zeros((1, 128), jnp.float32), jnp.ones((1, 128), jnp.float32)
    all_spans, all_shares = [], []
    for group in range(window // 8 - 1, -1, -1):
        all_spans.insert(0, spans[group * 8 : group * 8 + 8] + span)
        all_shares.insert(0, shares[group * 8 : group * 8 + 8] * share)
        span, share = all_spans[0][0:1], all_shares[0][0:1]
    spans = jnp.concatenate(all_spans, 0)[:, 0:1]
    shares = jnp.concatenate(all_shares, 0)[:, 0:1]
    for slot in range(4):
        left = jnp.exp(-(spans * part_of(rate, slot))) * shares
        if slot == 0:
            reach[...] = left
        driven[slot] = left * part_of(admittance, slot)


def recurrence_kernel(own, direct, paired, factors, admittance, partial, first, drive):
    window, unit = own.shape
    row, half = lax.axis_index("row"), lax.axis_index("tm") % 2
    gain = admittance[:, pl.ds(pl.multiple_of((row * 2 + half) * unit, unit), unit)]
    total = (
        own[...].astype(jnp.float32)
        + direct[...].astype(jnp.float32)
        + paired[...].astype(jnp.float32)
    )
    state = factors[0] * total
    for slot, shift in ((1, 1), (2, 2), (3, 4)):
        state = state + factors[slot] * pltpu.roll(state, window - shift, 0)
    carry = jnp.zeros((1, unit), jnp.float32)
    for group in range(window // 8 - 1, -1, -1):
        rows = slice(group * 8, group * 8 + 8)
        block = state[rows] + factors[4, rows, :] * carry
        partial[rows, :] = block
        carry = block[0:1]
        if group * 8 == HALO:
            first[...] = jnp.broadcast_to(carry, first.shape)
    drive[...] = (gain * partial[...]).astype(drive.dtype)


def finish_kernel(incoming, partial, reach, mine, theirs, states):
    window, unit = states.shape
    length = mine.shape[1]
    half = lax.axis_index("tm") % 2
    first = pl.multiple_of(HALO + half * length, HALO)
    second = pl.multiple_of(HALO + (1 - half) * length, HALO)
    states[...] = partial[...] + reach[...] * incoming[0:1, :]
    mine[...] = states[pl.ds(first, length), :].T
    theirs[...] = states[pl.ds(second, length), :].T


def reconstruct_kernel(slots, places, stage, *refs):
    count = len(slots)
    drives, incoming, kernels = (refs[i * count : (i + 1) * count] for i in range(3))
    kernels = list(zip(kernels, places))
    driven, *refs = refs[3 * count :]
    if stage == "last":
        before, keep, send, steps, lagged = refs
    elif stage == "next":
        before, total, steps, lagged = refs
    else:
        total, steps, lagged = refs
    lags, width, _ = lagged.shape
    unit = drives[0].shape[1]
    for index, slot in enumerate(slots):
        steps[:, index * unit : index * unit + unit] = (
            drives[index][...].astype(jnp.float32) + driven[slot] * incoming[index][0:1, :]
        )
    for lag in range(lags):
        lagged[lag] = steps[HALO - lag : HALO - lag + width, :].astype(jnp.bfloat16)
    added = None if stage == "first" else before[...]
    for index, (kernel, at) in enumerate(kernels):
        rows = kernel.shape[0] // lags
        for lag in range(lags):
            term = lax.dot_general(
                kernel[lag * rows : lag * rows + rows, at * unit : at * unit + unit],
                lagged[lag, :, index * unit : index * unit + unit],
                (((1,), (1,)), ((), ())),
                preferred_element_type=jnp.float32,
            )
            added = term if added is None else added + term
    if stage == "last":
        length = width // 2
        odd = lax.axis_index("tm") % 2 == 1
        keep[...] = jnp.where(odd, added[:, length:], added[:, :length])
        send[...] = jnp.where(odd, added[:, :length], added[:, length:]).astype(send.dtype)
    else:
        total[...] = added


def call(kernel, name, in_specs, out_specs, out_shape, scratch, flops, moved):
    return pl.pallas_call(
        kernel,
        in_specs=in_specs,
        out_specs=out_specs,
        out_shape=out_shape,
        scratch_shapes=scratch,
        cost_estimate=pl.CostEstimate(flops=flops, bytes_accessed=moved, transcendentals=0),
        compiler_params=pltpu.CompilerParams(vmem_limit_bytes=VMEM_BYTES),
        name=name,
    )


def paired(
    traces,
    weights,
    pattern,
    cluster,
    element_damping_rate,
    local_step_length,
    housing_keep_share,
    admittance,
):
    rows, length = traces.shape
    lags = weights.shape[0]
    window = HALO + 2 * length
    unit = rows // 2
    half = lax.axis_index("tm") % 2
    odd = half == 1
    f32, bf16 = jnp.float32, jnp.bfloat16
    tm_count = lax.axis_size("tm")
    swap = [(i, i ^ 1) for i in range(tm_count)]
    near = [(i, i + 1 if i % 2 else i - 1) for i in range(tm_count)]
    near = [(i, j) for i, j in near if 0 <= j < tm_count]
    far = [(i, i + 2 if i % 2 else i - 2) for i in range(tm_count)]
    far = [(i, j) for i, j in far if 0 <= j < tm_count]
    vmem = pl.BlockSpec(memory_space=pltpu.VMEM)

    hbm = pl.BlockSpec(memory_space=pltpu.HBM)
    barrier = lax.optimization_barrier

    def held(array):
        return pltpu.with_memory_space_constraint(array, pltpu.HBM)

    edge, clocks, columns, bits, own = call(
        setup_kernel,
        "setup",
        [hbm] * 5,
        [vmem] * 5,
        [
            jax.ShapeDtypeStruct((HALO, rows + 128), f32),
            jax.ShapeDtypeStruct((8, length), f32),
            jax.ShapeDtypeStruct((rows, 8), jnp.int32),
            jax.ShapeDtypeStruct((1, cluster.shape[0]), jnp.int32),
            jax.ShapeDtypeStruct((length, rows), bf16),
        ],
        [
            pltpu.VMEM((rows, length), bf16),
            pltpu.VMEM((length, rows + 128), f32),
            pltpu.VMEM(pattern.shape, jnp.int32),
            pltpu.VMEM((1, cluster.shape[0]), jnp.int32),
            pltpu.SemaphoreType.DMA((5,)),
        ],
        rows * length * 4,
        rows * length * 2,
    )(
        held(traces),
        held(local_step_length[None]),
        held(housing_keep_share[None]),
        held(pattern),
        held(cluster[None]),
    )
    partner_clocks = lax.ppermute(clocks, "tm", swap)
    partner = lax.ppermute(own, "tm", swap)
    got_near = lax.ppermute(edge, "tm", near)
    got_far = lax.ppermute(edge, "tm", far)

    strip = jax.ShapeDtypeStruct((window, unit), bf16)
    share_bytes = lags * rows * unit * 2
    share_flops = 2 * lags * rows * unit * window

    def chosen(slots, columns):
        return call(
            functools.partial(mask_kernel, slots),
            "mask",
            [vmem] * 2 + [hbm],
            vmem,
            pltpu.VMEM((lags * rows, len(slots) * unit), bf16),
            [pltpu.VMEM((rows, 128), jnp.int32), pltpu.SemaphoreType.DMA((len(slots), lags))],
            share_bytes,
            share_bytes,
        )(columns, bits, weights)

    def correlated(kernels):
        return call(
            correlate_kernel,
            "correlate",
            [vmem] * 5,
            [vmem] * 2,
            [strip, pltpu.VMEM((window, lags * rows), bf16)],
            [pltpu.VMEM((window + HALO, rows), f32)],
            share_flops,
            share_bytes // 2,
        )(own, partner, got_near, got_far, kernels)

    def correlated_again(lagged, kernels):
        count = kernels.shape[1] // unit
        return call(
            correlate_again_kernel,
            "correlate",
            [vmem] * 2,
            [vmem] * count,
            [strip] * count,
            [],
            share_flops * count,
            share_bytes * count // 2,
        )(lagged, kernels)

    def added(mine, theirs):
        return call(
            pair_kernel, "pair", [vmem] * 2, vmem, strip, [], window * unit, window * unit * 6
        )(mine, theirs)

    def over_row(array, by):
        return lax.ppermute(array, "row", [(i, i ^ by) for i in range(4)])

    def factored(clocks):
        full = jax.ShapeDtypeStruct((window, unit), f32)
        return call(
            factors_kernel,
            "factors",
            [vmem] * 6,
            [vmem] * 3,
            [
                jax.ShapeDtypeStruct((5, window, unit), f32),
                full,
                jax.ShapeDtypeStruct((4, window, unit), f32),
            ],
            [pltpu.VMEM((window, 8), f32)],
            window * unit * 100,
            window * unit * 40,
        )(
            clocks,
            partner_clocks,
            got_near,
            got_far,
            element_damping_rate[None],
            admittance[None],
        )

    def recurrence(terms, factors):
        return call(
            recurrence_kernel,
            "recurrence",
            [vmem] * 5,
            [vmem] * 3,
            [
                jax.ShapeDtypeStruct((window, unit), f32),
                jax.ShapeDtypeStruct((8, unit), f32),
                strip,
            ],
            [],
            window * unit * 20,
            window * unit * 30,
        )(*terms, factors, admittance[None])

    def finished(partial, incoming, reach):
        return call(
            finish_kernel,
            "finish",
            [vmem] * 3,
            [vmem] * 2,
            [jax.ShapeDtypeStruct((unit, length), f32)] * 2,
            [pltpu.VMEM((window, unit), f32)],
            window * unit * 10,
            window * unit * 16,
        )(incoming, partial, reach)

    def reconstructed(stage, slots, units, driven, *before):
        count = len(slots)
        drives, incoming, kernels, places = zip(*units)
        out_shape = jax.ShapeDtypeStruct((rows, 2 * length), f32)
        if stage == "last":
            out_shape = [
                jax.ShapeDtypeStruct((rows, length), f32),
                jax.ShapeDtypeStruct((rows, length), bf16),
            ]
        return call(
            functools.partial(reconstruct_kernel, slots, places, stage),
            "reconstruct",
            [vmem] * (3 * count + 1 + len(before)),
            [vmem] * 2 if stage == "last" else vmem,
            out_shape,
            [
                pltpu.VMEM((window, count * unit), f32),
                pltpu.VMEM((lags, 2 * length, count * unit), bf16),
            ],
            share_flops * count,
            share_bytes * count // 2,
        )(*drives, *incoming, *kernels, driven, *before)

    first_kernels = chosen((3,), columns)
    o3, lagged = correlated(first_kernels)
    s3 = over_row(o3, 1)
    later, _ = barrier((columns, o3))
    middle_kernels = chosen((2, 1), later)
    o2, o1 = correlated_again(lagged, middle_kernels)
    pair = added(o2, s3)
    paired = over_row(pair, 2)
    later, _ = barrier((columns, pair))
    last_kernels = chosen((0,), later)
    (o0,) = correlated_again(lagged, last_kernels)
    direct = over_row(o1, 1)
    factors, reach, driven = factored(clocks)
    partial, first, d0 = recurrence((o0, direct, paired), factors)
    d2 = over_row(d0, 2)
    d1 = over_row(d0, 1)
    d3 = over_row(d2, 1)
    i0 = lax.ppermute(first, "tm", [(i, i - 2) for i in range(2, tm_count)])
    i2 = over_row(i0, 2)
    i1 = over_row(i0, 1)
    mine, theirs = finished(partial, i0, reach)
    theirs = lax.ppermute(theirs, "tm", swap)
    near_units = [(d0, i0, last_kernels, 0), (d1, i1, middle_kernels, 1)]
    total = reconstructed("first", (0, 1), near_units, driven)
    late, _ = barrier((i2, total))
    i3 = over_row(late, 1)
    total = reconstructed("next", (2,), [(d2, i2, middle_kernels, 0)], driven, total)
    keep, send = reconstructed("last", (3,), [(d3, i3, first_kernels, 0)], driven, total)
    pressure = keep + lax.ppermute(send, "tm", swap).astype(f32)
    state = jnp.where(
        odd, jnp.concatenate([theirs, mine], 0), jnp.concatenate([mine, theirs], 0)
    )
    return (state, pressure.astype(bf16))


def local(traces, weights, pattern, *rest):
    rows, length = traces.shape
    fits = (
        lax.axis_size("row") == 4
        and lax.axis_size("tm") == 4
        and length == 128
        and rows % 256 == 0
        and weights.shape[0] <= 8
        and pattern.shape[1] <= 32
    )
    return (paired if fits else general)(traces, weights, pattern, *rest)


def solution(mesh):
    placed = (P("row", ("group", "tm")), P(None, "row", None), P(), P(), P(), P("tm"), P("tm"), P())
    return jax.shard_map(
        local,
        mesh=mesh,
        in_specs=placed,
        out_specs=(P("row", ("group", "tm")), P("row", ("group", "tm"))),
        check_vma=False,
    )
```

```python
import functools

import jax
import jax.numpy as jnp
from jax import lax
from jax.experimental import pallas as pl
from jax.experimental.pallas import tpu as pltpu
from jax.sharding import PartitionSpec as P

HALO = 8
VMEM_BYTES = 20 << 20


def carried_in(array, axis, join, neutral):
    count = lax.axis_size(axis)
    place = lax.axis_index(axis)
    ahead = count - 1 - place
    gathered = jax.tree.map(
        lambda a, kind: lax.all_gather(a.astype(kind), axis),
        array,
        jax.tree.map(lambda a: jnp.bfloat16 if a.dtype == jnp.float32 else a.dtype, array),
    )
    state = jax.tree.map(lambda a, e: jnp.zeros_like(a) + jnp.asarray(e, a.dtype), array, neutral)

    def one(hop, state):
        source = count - 1 - hop
        return join(
            state,
            jax.tree.map(
                lambda a, own: lax.dynamic_index_in_dim(a, source, 0, False).astype(own.dtype),
                gathered,
                array,
            ),
        )

    return lax.fori_loop(0, ahead, one, state)


def from_behind(array, axis, by):
    count = lax.axis_size(axis)
    pairs = [(i, i + by) for i in range(count) if 0 <= i + by < count]
    return lax.ppermute(array, axis, pairs)


def lag_kernels(weights, pattern, cluster, first_row):
    local_rows = weights.shape[1]
    own_labels = lax.dynamic_slice_in_dim(cluster, first_row, local_rows, 0)
    labels = jnp.arange(pattern.shape[1], dtype=jnp.int32)
    row_onehot = (own_labels[:, None] == labels[None, :]).astype(jnp.bfloat16)
    column_onehot = (labels[:, None] == cluster[None, :]).astype(jnp.bfloat16)
    kernels = []
    for lag_index in range(weights.shape[0]):
        picked = jnp.dot(
            row_onehot, pattern[lag_index].astype(jnp.bfloat16), preferred_element_type=jnp.float32
        )
        table = jnp.dot(
            picked.astype(jnp.bfloat16), column_onehot, preferred_element_type=jnp.float32
        )
        kernels.append(weights[lag_index] * table.astype(jnp.bfloat16))
    return kernels


def correlate(kernels, extended):
    length = extended.shape[1] - len(kernels) + 1
    running = None
    for lag_index in range(len(kernels)):
        product_term = lax.dot_general(
            kernels[lag_index],
            extended[:, lag_index : lag_index + length],
            (((0,), (0,)), ((), ())),
            preferred_element_type=jnp.float32,
        )
        running = product_term if running is None else running + product_term
    return running


def reconstruct(kernels, extended):
    number_of_lags = len(kernels)
    length = extended.shape[1] - number_of_lags + 1
    running = None
    for lag_index in range(number_of_lags):
        offset = number_of_lags - 1 - lag_index
        product_term = jnp.dot(
            kernels[lag_index],
            extended[:, offset : offset + length],
            preferred_element_type=jnp.float32,
        )
        running = product_term if running is None else running + product_term
    return running


def chain_step(earlier, later):
    return (later[0] * earlier[0], later[1] + later[0] * earlier[1])


def block_recurrence(keep_fraction, inflow):
    def advance(carry, pieces):
        kept_now, state_now = carry
        keep, more = pieces
        state_now = keep * state_now + more
        kept_now = keep * kept_now
        return ((kept_now, state_now), (kept_now, state_now))

    elements = keep_fraction.shape[0]
    start = (jnp.ones((elements,), jnp.float32), jnp.zeros((elements,), jnp.float32))
    _, outputs = lax.scan(advance, start, (keep_fraction.T, inflow.T), reverse=True)
    return (outputs[0].T, outputs[1].T)


def general(
    traces,
    weights,
    pattern,
    cluster,
    element_damping_rate,
    local_step_length,
    housing_keep_share,
    admittance,
):
    local_rows = traces.shape[0]
    length = traces.shape[1]
    number_of_lags = weights.shape[0]
    first_row = lax.axis_index("row") * local_rows
    kernels = lag_kernels(weights, pattern, cluster, first_row)
    trailing = from_behind(traces[:, : number_of_lags - 1], "tm", -1)
    extended = jnp.concatenate([traces, trailing], 1)
    adjoint_sum = lax.psum(correlate(kernels, extended).astype(jnp.bfloat16), "row").astype(
        jnp.float32
    )
    spent = element_damping_rate[:, None] * local_step_length[None, :]
    keep_fraction = jnp.exp(-spent) * housing_keep_share[None, :]
    inflow = jnp.sqrt(-jnp.expm1(-2.0 * spent)) * adjoint_sum
    retained, partial_state = block_recurrence(keep_fraction, inflow)
    neutral = (jnp.ones_like(retained[:, 0]), jnp.zeros_like(partial_state[:, 0]))
    incoming = carried_in((retained[:, 0], partial_state[:, 0]), "tm", chain_step, neutral)
    state = partial_state + retained * incoming[1][:, None]
    driving = (admittance[:, None] * state).astype(jnp.bfloat16)
    leading = from_behind(driving[:, length - number_of_lags + 1 :], "tm", 1)
    pressure = reconstruct(kernels, jnp.concatenate([leading, driving], 1))
    state = lax.dynamic_slice_in_dim(state, first_row, local_rows, 0)
    return (state, pressure.astype(jnp.bfloat16))


def setup_kernel(
    traces_in,
    length_in,
    share_in,
    pattern_in,
    cluster_in,
    edge,
    clocks,
    columns,
    bits,
    own,
    traces,
    turned,
    pattern,
    cluster,
    ready,
):
    rows, length = traces.shape
    lags, kinds, _ = pattern.shape
    row, odd = lax.axis_index("row"), lax.axis_index("tm") % 2
    moves = (
        (traces_in, traces),
        (length_in, clocks.at[0:1, :]),
        (share_in, clocks.at[1:2, :]),
        (pattern_in, pattern),
        (cluster_in, cluster),
    )
    clocks[...] = jnp.zeros_like(clocks)
    copies = [
        pltpu.make_async_copy(source, target, ready.at[index])
        for index, (source, target) in enumerate(moves)
    ]
    for copy in copies:
        copy.start()
    for copy in copies:
        copy.wait()
    turned[:, 0:rows] = traces[...].astype(jnp.float32).T
    turned[:, rows:] = jnp.zeros((length, 128), jnp.float32)
    turned[:, rows : rows + 8] = clocks[...].T
    edge[...] = turned[pl.ds(pl.multiple_of(odd * (length - HALO), HALO), HALO), :]
    own[...] = turned[:, 0:rows].astype(jnp.bfloat16)

    bits[...] = jnp.int32(1) << cluster[...]
    labels = cluster[:, pl.ds(pl.multiple_of(row * rows, rows), rows)]
    hit = lax.broadcasted_iota(jnp.int32, (kinds, rows), 0) == labels
    places = lax.broadcasted_iota(jnp.int32, (kinds, pattern.shape[2]), 1)
    found = []
    for lag in range(lags):
        word = (pattern[lag] << places).sum(1, keepdims=True)
        found.append(jnp.where(hit, word, 0).sum(0, keepdims=True))
    found = jnp.concatenate(found + [jnp.zeros((8 - lags, rows), jnp.int32)], 0)
    columns[...] = found.T


def mask_kernel(slots, columns, bits, weights, kernels, spread, arrived):
    lags, rows, _ = weights.shape
    unit = kernels.shape[1] // len(slots)
    row, half = lax.axis_index("row"), lax.axis_index("tm") % 2

    def start_of(slot):
        return pl.multiple_of((jnp.bitwise_xor(row, slot) * 2 + half) * unit, unit)

    def fetch(lag, index):
        return pltpu.make_async_copy(
            weights.at[lag, :, pl.ds(start_of(slots[index]), unit)],
            kernels.at[pl.ds(lag * rows, rows), pl.ds(index * unit, unit)],
            arrived.at[index, lag],
        )

    blocks = [(lag, index) for lag in range(lags) for index in range(len(slots))]
    for block in blocks:
        fetch(*block).start()
    picked = [bits[:, pl.ds(start_of(slot), unit)] for slot in slots]
    for lag, index in blocks:
        if index == 0:
            spread[...] = jnp.broadcast_to(columns[:, lag : lag + 1], (rows, 128))
        fetch(lag, index).wait()
        for top in range(0, rows, 128):
            word = spread[top : top + 128, :]
            place = slice(lag * rows + top, lag * rows + top + 128)
            for at in range(0, unit, 128):
                part = slice(index * unit + at, index * unit + at + 128)
                weight = kernels[place, part]
                keep = (word & picked[index][:, at : at + 128]) != 0
                kernels[place, part] = jnp.where(keep, weight, jnp.zeros_like(weight))


def correlate_kernel(own, partner, near, far, kernels, *refs):
    *outs, lagged, steps = refs
    length, rows = own.shape
    window = lagged.shape[0]
    lags = lagged.shape[1] // rows
    half = lax.axis_index("tm") % 2
    odd = half == 1
    first = pl.multiple_of(HALO + half * length, HALO)
    second = pl.multiple_of(HALO + (1 - half) * length, HALO)
    steps[0:HALO, :] = jnp.where(odd, far[:, 0:rows], near[:, 0:rows])
    steps[window : window + HALO, :] = jnp.where(odd, near[:, 0:rows], far[:, 0:rows])
    steps[pl.ds(first, length), :] = own[...].astype(jnp.float32)
    steps[pl.ds(second, length), :] = partner[...].astype(jnp.float32)
    for lag in range(lags):
        part = slice(lag * rows, lag * rows + rows)
        lagged[:, part] = steps[lag : lag + window, :].astype(jnp.bfloat16)
    multiply(lagged, kernels, outs)


def mask_correlate_kernel(slots, lagged, columns, bits, weights, *refs):
    *outs, kernels, spread, arrived = refs
    mask_kernel(slots, columns, bits, weights, kernels, spread, arrived)
    multiply(lagged, kernels, outs)


def multiply(lagged, kernels, outs):
    unit = outs[0].shape[1]
    for index, out in enumerate(outs):
        out[...] = jnp.dot(
            lagged[...],
            kernels[:, index * unit : index * unit + unit],
            preferred_element_type=jnp.float32,
        ).astype(out.dtype)


def pair_kernel(mine, theirs, out):
    out[...] = (mine[...].astype(jnp.float32) + theirs[...].astype(jnp.float32)).astype(out.dtype)


def one_less_exp(y):
    series = jnp.ones_like(y)
    for k in range(9, 1, -1):
        series = 1.0 - series * y * (1.0 / k)
    return jnp.where(y < 0.5, y * series, 1.0 - jnp.exp(-y))


def factors_kernel(
    clocks, partner_clocks, near, far, rate, out, columns
):
    _, window, unit = out.shape
    length = clocks.shape[1]
    rows = near.shape[1] - 128
    row, half = lax.axis_index("row"), lax.axis_index("tm") % 2
    first = pl.multiple_of(HALO + half * length, HALO)
    second = pl.multiple_of(HALO + (1 - half) * length, HALO)
    columns[0:HALO, :] = jnp.where(half == 1, far[:, rows : rows + 8], near[:, rows : rows + 8])
    columns[pl.ds(first, length), :] = clocks[...].T
    columns[pl.ds(second, length), :] = partner_clocks[...].T

    start = pl.multiple_of((row * 2 + half) * unit, unit)
    index = lax.broadcasted_iota(jnp.int32, (window, unit), 0) & 7
    spent = columns[:, 0:1] * rate[:, pl.ds(start, unit)]
    out[0] = jnp.sqrt(one_less_exp(2.0 * spent))
    kept = jnp.exp(-spent) * columns[:, 1:2]
    for slot, shift in ((1, 1), (2, 2), (3, 4)):
        inside = index < 8 - shift
        out[slot] = jnp.where(inside, kept, 0.0)
        kept = jnp.where(inside, kept * pltpu.roll(kept, window - shift, 0), kept)
    out[4] = kept


def reach_kernel(columns, rate, admittance, reach, driven):
    _, window, unit = driven.shape
    row, half = lax.axis_index("row"), lax.axis_index("tm") % 2

    def part_of(array, slot):
        start = pl.multiple_of((jnp.bitwise_xor(row, slot) * 2 + half) * unit, unit)
        return array[:, pl.ds(start, unit)]

    spans = jnp.broadcast_to(columns[:, 0:1], (window, 128))
    shares = jnp.broadcast_to(columns[:, 1:2], (window, 128))
    inside = lax.broadcasted_iota(jnp.int32, (window, 128), 0) & 7
    for shift in (1, 2, 4):
        later = pltpu.roll(spans, window - shift, 0)
        spans = jnp.where(inside < 8 - shift, spans + later, spans)
        later = pltpu.roll(shares, window - shift, 0)
        shares = jnp.where(inside < 8 - shift, shares * later, shares)
    span, share = jnp.zeros((1, 128), jnp.float32), jnp.ones((1, 128), jnp.float32)
    all_spans, all_shares = [], []
    for group in range(window // 8 - 1, -1, -1):
        all_spans.insert(0, spans[group * 8 : group * 8 + 8] + span)
        all_shares.insert(0, shares[group * 8 : group * 8 + 8] * share)
        span, share = all_spans[0][0:1], all_shares[0][0:1]
    spans = jnp.concatenate(all_spans, 0)[:, 0:1]
    shares = jnp.concatenate(all_shares, 0)[:, 0:1]
    for slot in range(4):
        left = jnp.exp(-(spans * part_of(rate, slot))) * shares
        if slot == 0:
            reach[...] = left
        driven[slot] = left * part_of(admittance, slot)


def recurrence_kernel(own, direct, paired, factors, admittance, partial, first, drive):
    window, unit = own.shape
    row, half = lax.axis_index("row"), lax.axis_index("tm") % 2
    gain = admittance[:, pl.ds(pl.multiple_of((row * 2 + half) * unit, unit), unit)]
    total = (
        own[...].astype(jnp.float32)
        + direct[...].astype(jnp.float32)
        + paired[...].astype(jnp.float32)
    )
    state = factors[0] * total
    for slot, shift in ((1, 1), (2, 2), (3, 4)):
        state = state + factors[slot] * pltpu.roll(state, window - shift, 0)
    carry = jnp.zeros((1, unit), jnp.float32)
    waiting = None
    for group in range(window // 8 - 1, -1, -1):
        rows = slice(group * 8, group * 8 + 8)
        block = state[rows] + factors[4, rows, :] * carry
        partial[rows, :] = block
        carry = block[0:1]
        if group * 8 == HALO:
            first[...] = jnp.broadcast_to(carry, first.shape)
        if waiting is not None:
            both = jnp.concatenate([gain * block, waiting], 0)
            drive[group * 8 : group * 8 + 16, :] = both.astype(drive.dtype)
            waiting = None
        elif group % 2 == 0:
            drive[rows, :] = (gain * block).astype(drive.dtype)
        else:
            waiting = gain * block


def finish_kernel(incoming, partial, reach, mine, theirs, states):
    window, unit = states.shape
    length = mine.shape[1]
    half = lax.axis_index("tm") % 2
    first = pl.multiple_of(HALO + half * length, HALO)
    second = pl.multiple_of(HALO + (1 - half) * length, HALO)
    states[...] = partial[...] + reach[...] * incoming[0:1, :]
    mine[...] = states[pl.ds(first, length), :].T
    theirs[...] = states[pl.ds(second, length), :].T


def reconstruct_kernel(slots, places, stage, *refs):
    count = len(slots)
    drives, incoming, kernels = (refs[i * count : (i + 1) * count] for i in range(3))
    kernels = list(zip(kernels, places))
    driven, *refs = refs[3 * count :]
    if stage == "last":
        before, keep, send, steps, lagged = refs
    elif stage == "next":
        before, total, steps, lagged = refs
    else:
        total, steps, lagged = refs
    lags, width, _ = lagged.shape
    unit = drives[0].shape[1]
    for index, slot in enumerate(slots):
        steps[:, index * unit : index * unit + unit] = (
            drives[index][...].astype(jnp.float32) + driven[slot] * incoming[index][0:1, :]
        )
    for lag in range(lags):
        lagged[lag] = steps[HALO - lag : HALO - lag + width, :].astype(jnp.bfloat16)
    added = None if stage == "first" else before[...]
    for index, (kernel, at) in enumerate(kernels):
        rows = kernel.shape[0] // lags
        for lag in range(lags):
            term = lax.dot_general(
                kernel[lag * rows : lag * rows + rows, at * unit : at * unit + unit],
                lagged[lag, :, index * unit : index * unit + unit],
                (((1,), (1,)), ((), ())),
                preferred_element_type=jnp.float32,
            )
            added = term if added is None else added + term
    if stage == "last":
        length = width // 2
        odd = lax.axis_index("tm") % 2 == 1
        keep[...] = jnp.where(odd, added[:, length:], added[:, :length])
        send[...] = jnp.where(odd, added[:, :length], added[:, length:]).astype(send.dtype)
    else:
        total[...] = added


def call(kernel, name, in_specs, out_specs, out_shape, scratch, flops, moved):
    return pl.pallas_call(
        kernel,
        in_specs=in_specs,
        out_specs=out_specs,
        out_shape=out_shape,
        scratch_shapes=scratch,
        cost_estimate=pl.CostEstimate(flops=flops, bytes_accessed=moved, transcendentals=0),
        compiler_params=pltpu.CompilerParams(vmem_limit_bytes=VMEM_BYTES),
        name=name,
    )


def paired(
    traces,
    weights,
    pattern,
    cluster,
    element_damping_rate,
    local_step_length,
    housing_keep_share,
    admittance,
):
    rows, length = traces.shape
    lags = weights.shape[0]
    window = HALO + 2 * length
    unit = rows // 2
    half = lax.axis_index("tm") % 2
    odd = half == 1
    f32, bf16 = jnp.float32, jnp.bfloat16
    tm_count = lax.axis_size("tm")
    swap = [(i, i ^ 1) for i in range(tm_count)]
    near = [(i, i + 1 if i % 2 else i - 1) for i in range(tm_count)]
    near = [(i, j) for i, j in near if 0 <= j < tm_count]
    far = [(i, i + 2 if i % 2 else i - 2) for i in range(tm_count)]
    far = [(i, j) for i, j in far if 0 <= j < tm_count]
    vmem = pl.BlockSpec(memory_space=pltpu.VMEM)

    hbm = pl.BlockSpec(memory_space=pltpu.HBM)
    barrier = lax.optimization_barrier

    def held(array):
        return pltpu.with_memory_space_constraint(array, pltpu.HBM)

    edge, clocks, columns, bits, own = call(
        setup_kernel,
        "setup",
        [hbm] * 5,
        [vmem] * 5,
        [
            jax.ShapeDtypeStruct((HALO, rows + 128), f32),
            jax.ShapeDtypeStruct((8, length), f32),
            jax.ShapeDtypeStruct((rows, 8), jnp.int32),
            jax.ShapeDtypeStruct((1, cluster.shape[0]), jnp.int32),
            jax.ShapeDtypeStruct((length, rows), bf16),
        ],
        [
            pltpu.VMEM((rows, length), bf16),
            pltpu.VMEM((length, rows + 128), f32),
            pltpu.VMEM(pattern.shape, jnp.int32),
            pltpu.VMEM((1, cluster.shape[0]), jnp.int32),
            pltpu.SemaphoreType.DMA((5,)),
        ],
        rows * length * 4,
        rows * length * 2,
    )(
        held(traces),
        held(local_step_length[None]),
        held(housing_keep_share[None]),
        held(pattern),
        held(cluster[None]),
    )
    partner_clocks = lax.ppermute(clocks, "tm", swap)
    partner = lax.ppermute(own, "tm", swap)
    got_near = lax.ppermute(edge, "tm", near)
    got_far = lax.ppermute(edge, "tm", far)

    strip = jax.ShapeDtypeStruct((window, unit), bf16)
    share_bytes = lags * rows * unit * 2
    share_flops = 2 * lags * rows * unit * window

    def chosen(slots, columns):
        return call(
            functools.partial(mask_kernel, slots),
            "mask",
            [vmem] * 2 + [hbm],
            vmem,
            pltpu.VMEM((lags * rows, len(slots) * unit), bf16),
            [pltpu.VMEM((rows, 128), jnp.int32), pltpu.SemaphoreType.DMA((len(slots), lags))],
            share_bytes,
            share_bytes,
        )(columns, bits, weights)

    def correlated(kernels):
        return call(
            correlate_kernel,
            "correlate",
            [vmem] * 5,
            [vmem] * 2,
            [strip, pltpu.VMEM((window, lags * rows), bf16)],
            [pltpu.VMEM((window + HALO, rows), f32)],
            share_flops,
            share_bytes // 2,
        )(own, partner, got_near, got_far, kernels)

    def correlated_again(lagged, slots, columns):
        count = len(slots)
        return call(
            functools.partial(mask_correlate_kernel, slots),
            "correlate",
            [vmem] * 3 + [hbm],
            [vmem] * (count + 1),
            [strip] * count + [pltpu.VMEM((lags * rows, count * unit), bf16)],
            [pltpu.VMEM((rows, 128), jnp.int32), pltpu.SemaphoreType.DMA((count, lags))],
            share_flops * count,
            share_bytes * count,
        )(lagged, columns, bits, weights)

    def added(mine, theirs):
        return call(
            pair_kernel, "pair", [vmem] * 2, vmem, strip, [], window * unit, window * unit * 6
        )(mine, theirs)

    def over_row(array, by):
        return lax.ppermute(array, "row", [(i, i ^ by) for i in range(4)])

    def factored(clocks):
        return call(
            factors_kernel,
            "factors",
            [vmem] * 5,
            [vmem] * 2,
            [
                jax.ShapeDtypeStruct((5, window, unit), f32),
                jax.ShapeDtypeStruct((window, 8), f32),
            ],
            [],
            window * unit * 80,
            window * unit * 20,
        )(clocks, partner_clocks, got_near, got_far, element_damping_rate[None])

    def reaching(columns):
        return call(
            reach_kernel,
            "reach",
            [vmem] * 3,
            [vmem] * 2,
            [
                jax.ShapeDtypeStruct((window, unit), f32),
                jax.ShapeDtypeStruct((4, window, unit), f32),
            ],
            [],
            window * unit * 40,
            window * unit * 20,
        )(columns, element_damping_rate[None], admittance[None])

    def recurrence(terms, factors):
        return call(
            recurrence_kernel,
            "recurrence",
            [vmem] * 5,
            [vmem] * 3,
            [
                jax.ShapeDtypeStruct((window, unit), f32),
                jax.ShapeDtypeStruct((8, unit), f32),
                strip,
            ],
            [],
            window * unit * 20,
            window * unit * 30,
        )(*terms, factors, admittance[None])

    def finished(partial, incoming, reach):
        return call(
            finish_kernel,
            "finish",
            [vmem] * 3,
            [vmem] * 2,
            [jax.ShapeDtypeStruct((unit, length), f32)] * 2,
            [pltpu.VMEM((window, unit), f32)],
            window * unit * 10,
            window * unit * 16,
        )(incoming, partial, reach)

    def reconstructed(stage, slots, units, driven, *before):
        count = len(slots)
        drives, incoming, kernels, places = zip(*units)
        out_shape = jax.ShapeDtypeStruct((rows, 2 * length), f32)
        if stage == "last":
            out_shape = [
                jax.ShapeDtypeStruct((rows, length), f32),
                jax.ShapeDtypeStruct((rows, length), bf16),
            ]
        return call(
            functools.partial(reconstruct_kernel, slots, places, stage),
            "reconstruct",
            [vmem] * (3 * count + 1 + len(before)),
            [vmem] * 2 if stage == "last" else vmem,
            out_shape,
            [
                pltpu.VMEM((window, count * unit), f32),
                pltpu.VMEM((lags, 2 * length, count * unit), bf16),
            ],
            share_flops * count,
            share_bytes * count // 2,
        )(*drives, *incoming, *kernels, driven, *before)

    first_kernels = chosen((3,), columns)
    o3, lagged = correlated(first_kernels)
    s3 = over_row(o3, 1)
    later, _ = barrier((columns, o3))
    o2, o1, middle_kernels = correlated_again(lagged, (2, 1), later)
    pair = added(o2, s3)
    paired = over_row(pair, 2)
    later, _ = barrier((columns, pair))
    o0, last_kernels = correlated_again(lagged, (0,), later)
    direct = over_row(o1, 1)
    factors, step_columns = factored(clocks)
    partial, first, d0 = recurrence((o0, direct, paired), factors)
    late_columns, _ = barrier((step_columns, d0))
    reach, driven = reaching(late_columns)
    d2 = over_row(d0, 2)
    d1 = over_row(d0, 1)
    d3 = over_row(d2, 1)
    i0 = lax.ppermute(first, "tm", [(i, i - 2) for i in range(2, tm_count)])
    i2 = over_row(i0, 2)
    i1 = over_row(i0, 1)
    mine, theirs = finished(partial, i0, reach)
    theirs = lax.ppermute(theirs, "tm", swap)
    near_units = [(d0, i0, last_kernels, 0), (d1, i1, middle_kernels, 1)]
    total = reconstructed("first", (0, 1), near_units, driven)
    late, _ = barrier((i2, total))
    i3 = over_row(late, 1)
    total = reconstructed("next", (2,), [(d2, i2, middle_kernels, 0)], driven, total)
    keep, send = reconstructed("last", (3,), [(d3, i3, first_kernels, 0)], driven, total)
    pressure = keep + lax.ppermute(send, "tm", swap).astype(f32)
    state = jnp.where(
        odd, jnp.concatenate([theirs, mine], 0), jnp.concatenate([mine, theirs], 0)
    )
    return (state, pressure.astype(bf16))


def local(traces, weights, pattern, *rest):
    rows, length = traces.shape
    fits = (
        lax.axis_size("row") == 4
        and lax.axis_size("tm") == 4
        and length == 128
        and rows % 256 == 0
        and weights.shape[0] <= 8
        and pattern.shape[1] <= 32
    )
    return (paired if fits else general)(traces, weights, pattern, *rest)


def solution(mesh):
    placed = (P("row", ("group", "tm")), P(None, "row", None), P(), P(), P(), P("tm"), P("tm"), P())
    return jax.shard_map(
        local,
        mesh=mesh,
        in_specs=placed,
        out_specs=(P("row", ("group", "tm")), P("row", ("group", "tm"))),
        check_vma=False,
    )
```
